512 devices in a mesh: parts: 512 (over x, y, z, core).
Axes of the slice: x: 4, y: 8, z: 8, core: 2. Of those that a mesh axis runs over, the one named last changes fastest.
Arguments:
- flow_state: float32 [5, 64, 32768], P(None, None, 'parts'), may hold values from -2 to 14, as said below
- state_tangent: float32 [5, 64, 32768], P(None, None, 'parts'), may hold values from -6 to 6
- far_field: float32 [5], replicated, may hold values from -0.3 to 5, as said below
- coordinates: float32 [3, 52224], P(None, 'parts'), as said below
- damping: float32 [2], replicated, may hold values from 0.1 to 1
- face_neighbour: int32 [6, 32768], P(None, 'parts'), may hold values from 0 to 96, as said below
- element_nodes: int32 [8, 32768], P(None, 'parts'), may hold values from 0 to 152, as said below
- upper_sends: int32 [16384], P('parts'), may hold values from 0 to 63, as said below
- lower_sends: int32 [16384], P('parts'), may hold values from 0 to 63, as said below
- node_sends: int32 [26112], P('parts'), may hold values from 0 to 101, as said below
- shock_flags: int32 [32768], P('parts'), may hold values from 0 to 1, as said below
Outputs:
- residual: float32 [5, 64, 32768], P(None, None, 'parts')
- state_change: float32 [5, 64, 32768], P(None, None, 'parts')
- node_update: float32 [3, 52224], P(None, 'parts')
The draws below stay inside these ranges and needn't reach their ends.
Inputs may be any that keep to these rules, and one draw needn't show every extreme that they name: `flow_state`: density and pressure at each point lie in 0.5 to 2 and velocity components within 1 of (0, 0, 1.5). `far_field`: density and pressure lie in 0.8 to 1.2, velocity components within 0.2 of (0, 0, 1.5). `coordinates`: hexahedra stay valid: each element's trilinear map keeps a positive Jacobian at all points. `face_neighbour`: entry f of an element is a local element below 64, 64 + a halo slot below 32 (faces 0 and 1 only), or 96 for the far field; neighbours share the element's reference orientation. `element_nodes`: a local owned node below 102, or 102 + a halo slot of a node owned by the next partition. `upper_sends`: on each partition 32 distinct local elements. `lower_sends`: on each partition 32 distinct local elements. `node_sends`: on each partition 51 distinct owned nodes. `shock_flags`: at most 16 flagged elements in one partition, and some partition has exactly 16.
All inputs are finite; a program needn't handle non-finite values.
Results may differ from the reference program's by a relative error of at most 0.0003.
Values sent between devices are 32-bit elements; how exact they have to be, the bound alone decides.
No kernel may reach another device: no remote copies, remote signals or barrier semaphores. Data moves between devices by JAX's collectives and lax.ppermute only.
A program may use at most 128 MiB of HBM per device.

```python
import math
import jax
import jax.numpy as jnp
import numpy as np
from jax import lax

NT = 2
NN = 16
NW = 2
VARS = 5
QPTS = 64
EL = 64
HS = 32
NE = 32768
NH = 51
NO = 102
NNODE = 52224
FLAG_MAX = 16
N_PARTS = 512


def partition_orders(key, salt, length):
    partitions = NE // EL
    keys = jax.random.split(jax.random.fold_in(key, salt), partitions)
    return jax.vmap(lambda k: jax.random.permutation(k, length))(keys)


def mesh_layout(key):
    partitions = NE // EL
    element_order = partition_orders(key, 101, EL)
    node_order = partition_orders(key, 102, NO)
    lower_slots = partition_orders(key, 103, HS)
    upper_slots = partition_orders(key, 104, HS)
    node_slots = partition_orders(key, 105, NH)
    return (partitions, element_order, node_order, lower_slots, upper_slots, node_slots)


def element_columns(partitions, element_order):
    return (jnp.arange(partitions, dtype=jnp.int32)[:, None] * EL + element_order).reshape(-1)


def draw_face_neighbour(key, part):
    partitions, element_order, node_order, lower_slots, upper_slots, node_slots = mesh_layout(key)
    canonical = jnp.arange(EL, dtype=jnp.int32)
    column = canonical // HS
    rest = canonical % HS
    along = rest // NN
    across = rest % NN
    outside = EL + HS

    def beside(offset):
        return jnp.take(element_order, jnp.clip(canonical + offset, 0, EL - 1), axis=1)
    entries = [jnp.where(column > 0, beside(-HS), EL + jnp.take(lower_slots, rest, axis=1)), jnp.where(column < NW - 1, beside(HS), EL + jnp.take(upper_slots, rest, axis=1)), jnp.where(along > 0, beside(-NN), outside), jnp.where(along < NT - 1, beside(NN), outside), jnp.where(across > 0, beside(-1), outside), jnp.where(across < NN - 1, beside(1), outside)]
    stacked = jnp.stack([jnp.broadcast_to(e, (partitions, EL)) for e in entries]).astype(jnp.int32)
    return jnp.zeros((6, NE), jnp.int32).at[:, element_columns(partitions, element_order)].set(stacked.reshape(6, -1))


def draw_element_nodes(key, part):
    partitions, element_order, node_order, lower_slots, upper_slots, node_slots = mesh_layout(key)
    canonical = jnp.arange(EL, dtype=jnp.int32)
    column = canonical // HS
    rest = canonical % HS
    along = rest // NN
    across = rest % NN
    entries = []
    for k in range(8):
        target = (along + k // 2 % 2) * (NN + 1) + across + k % 2
        node_column = column + k // 4
        local_node = jnp.take(node_order, jnp.minimum(node_column * NH + target, NO - 1), axis=1)
        halo_node = NO + jnp.take(node_slots, target, axis=1)
        entries.append(jnp.where(node_column < NW, local_node, halo_node))
    stacked = jnp.stack(entries).astype(jnp.int32)
    return jnp.zeros((8, NE), jnp.int32).at[:, element_columns(partitions, element_order)].set(stacked.reshape(8, -1))


def sends_from(partitions, receiver_slots, sender_values, length):
    columns = (jnp.arange(partitions, dtype=jnp.int32)[:, None] * length + receiver_slots).reshape(-1)
    return jnp.zeros((partitions * length,), jnp.int32).at[columns].set(sender_values.reshape(-1).astype(jnp.int32))


def draw_upper_sends(key, part):
    partitions, element_order, node_order, lower_slots, upper_slots, node_slots = mesh_layout(key)
    return sends_from(partitions, jnp.roll(lower_slots, -1, axis=0), element_order[:, (NW - 1) * HS:], HS)


def draw_lower_sends(key, part):
    partitions, element_order, node_order, lower_slots, upper_slots, node_slots = mesh_layout(key)
    return sends_from(partitions, jnp.roll(upper_slots, 1, axis=0), element_order[:, :HS], HS)


def draw_node_sends(key, part):
    partitions, element_order, node_order, lower_slots, upper_slots, node_slots = mesh_layout(key)
    return sends_from(partitions, jnp.roll(node_slots, 1, axis=0), node_order[:, :NH], NH)


def draw_coordinates(key, part):
    partitions, element_order, node_order, lower_slots, upper_slots, node_slots = mesh_layout(key)
    canonical = jnp.arange(NO)
    column = (canonical // NH).astype(jnp.float32)
    rest = canonical % NH
    along = (rest // (NN + 1)).astype(jnp.float32)
    across = (rest % (NN + 1)).astype(jnp.float32)
    azimuth = 2.0 * math.pi / (partitions * NW) * (NW * jnp.arange(partitions, dtype=jnp.float32)[:, None] + column[None, :])
    radius = partitions * NW / (2.0 * math.pi) + 0.6 * across
    jitter_key = jax.random.fold_in(key, 106)
    jitter = 0.04 * jax.random.truncated_normal(jitter_key, -2.0, 2.0, (3, partitions, NO), jnp.float32)
    positions = jnp.stack([radius * jnp.cos(azimuth) + jitter[0], radius * jnp.sin(azimuth) + jitter[1], jnp.broadcast_to(along, (partitions, NO)) + jitter[2]])
    columns = (jnp.arange(partitions, dtype=jnp.int32)[:, None] * NO + node_order).reshape(-1)
    return jnp.zeros((3, NNODE), jnp.float32).at[:, columns].set(positions.reshape(3, -1))


def draw_shock_flags(key, part):
    partitions = NE // EL
    ranks = partition_orders(key, 107, EL)
    indices = jnp.arange(partitions, dtype=jnp.int32)
    lowest = FLAG_MAX * (partitions + 2 * indices) // (3 * partitions)
    counts = jax.random.randint(jax.random.fold_in(key, 108), (partitions,), lowest, FLAG_MAX + 1)
    fullest = jax.random.randint(jax.random.fold_in(key, 109), (), 0, partitions)
    counts = jnp.where(indices == fullest, FLAG_MAX, counts)
    return (ranks < counts[:, None]).astype(jnp.int32).reshape(-1)


def conserved(density, velocity, pressure):
    energy = pressure / 0.4 + 0.5 * density * jnp.sum(velocity * velocity, axis=0)
    return jnp.concatenate([density[None], density[None] * velocity, energy[None]], axis=0)


def draw_flow_state(key, part):
    keys = jax.random.split(jax.random.fold_in(key, 201), 3)
    point_shape = (64, NE)
    density = jnp.exp(jax.random.uniform(keys[0], point_shape, jnp.float32, math.log(0.5), math.log(2.0)))
    pressure = jnp.exp(jax.random.uniform(keys[1], point_shape, jnp.float32, math.log(0.5), math.log(2.0)))
    velocity = jnp.clip(0.5 * jax.random.normal(keys[2], (3,) + point_shape, jnp.float32), -1.0, 1.0)
    velocity = velocity + jnp.array([0.0, 0.0, 1.5], jnp.float32).reshape(3, 1, 1)
    return conserved(density, velocity, pressure)


def draw_far_field(key, part):
    keys = jax.random.split(jax.random.fold_in(key, 301), 3)
    density = jax.random.uniform(keys[0], (1,), jnp.float32, 0.8, 1.2)
    pressure = jax.random.uniform(keys[1], (1,), jnp.float32, 0.8, 1.2)
    velocity = jax.random.uniform(keys[2], (3, 1), jnp.float32, -0.2, 0.2) + jnp.array([0.0, 0.0, 1.5], jnp.float32).reshape(3, 1)
    return conserved(density, velocity, pressure).reshape(5)


def levels(own_key, extent, shards, least, high):
    def one(axis_at, shards_of):
        draws = jax.random.uniform(jax.random.fold_in(jax.random.fold_in(own_key, 6), axis_at), (shards_of,), jnp.float32, least / len(shards), high / len(shards))
        return jnp.repeat(jnp.exp(draws), extent[axis_at] // shards_of).reshape((-1,) + (1,) * (len(extent) - axis_at - 1))

    loudness = one(*shards[0])
    for cut in shards[1:]:
        loudness = loudness * one(*cut)
    return loudness


def noise(rng, dims, spread, bound, cuts=(), kind=jnp.bfloat16):
    values = jax.random.normal(rng, dims, jnp.float32) * spread
    if len(cuts) > 0:
        values = levels(rng, dims, cuts, -0.22, 0.18) * values
    return jnp.clip(values, min=-bound, max=bound).astype(kind)


def setup_inputs(seed: int = 0) -> dict:
    splits = jax.random.split(jax.random.key(seed), 12)
    return {
        "flow_state": draw_flow_state(jax.random.fold_in(splits[11], 71), 0),
        "state_tangent": noise(splits[1], (VARS, QPTS, NE), 1.0, 6.0, ((2, 512),), jnp.float32),
        "far_field": draw_far_field(jax.random.fold_in(splits[11], 71), 0),
        "coordinates": draw_coordinates(jax.random.fold_in(splits[11], 71), 0),
        "damping": jnp.clip(jnp.exp(jax.random.uniform(splits[4], (2,), jnp.float32, math.log(0.1), math.log(1.0))), 0.1, 1.0),
        "face_neighbour": draw_face_neighbour(jax.random.fold_in(splits[11], 71), 0),
        "element_nodes": draw_element_nodes(jax.random.fold_in(splits[11], 71), 0),
        "upper_sends": draw_upper_sends(jax.random.fold_in(splits[11], 71), 0),
        "lower_sends": draw_lower_sends(jax.random.fold_in(splits[11], 71), 0),
        "node_sends": draw_node_sends(jax.random.fold_in(splits[11], 71), 0),
        "shock_flags": draw_shock_flags(jax.random.fold_in(splits[11], 71), 0),
    }


GAMMA = 1.4
SOFTENING = 0.01
HIGHEST = lax.Precision.HIGHEST

def lobatto_tables():
    points = np.array([-1.0, -math.sqrt(0.2), math.sqrt(0.2), 1.0])
    weights = np.array([1.0, 5.0, 5.0, 1.0]) / 6.0
    derivative = np.zeros((4, 4))
    for a in range(4):
        for b in range(4):
            if a == b:
                derivative[a, b] = sum((1.0 / (points[a] - points[m]) for m in range(4) if m != a))
            else:
                numerator = 1.0
                denominator = 1.0
                for m in range(4):
                    if m != b:
                        denominator *= points[b] - points[m]
                        if m != a:
                            numerator *= points[a] - points[m]
                derivative[a, b] = numerator / denominator
    return (points, weights, derivative)

def shape_gradients():
    points = lobatto_tables()[0]
    gradients = np.zeros((3, 64, 8))
    for q in range(64):
        position = (q // 16, q // 4 % 4, q % 4)
        for k in range(8):
            corner_bits = (k // 4, k // 2 % 2, k % 2)
            for j in range(3):
                factor = 1.0
                for m in range(3):
                    orient = 1.0 if corner_bits[m] == 1 else -1.0
                    if m == j:
                        factor *= 0.5 * orient
                    else:
                        factor *= 0.5 * (1.0 + orient * points[position[m]])
                gradients[j, q, k] = factor
    return gradients

def edge_laplacian():
    matrix = np.zeros((8, 8))
    for k in range(8):
        matrix[k, k] = 3.0
        for b in range(3):
            matrix[k, k ^ 1 << b] = -1.0
    return matrix

def area_vectors(corners):
    gradients = jnp.asarray(shape_gradients(), jnp.float32)
    tangents = [[jnp.dot(gradients[j], corners[i], precision=HIGHEST, preferred_element_type=jnp.float32) for i in range(3)] for j in range(3)]
    result = []
    for j in range(3):
        first_edge = tangents[(j + 1) % 3]
        second = tangents[(j + 2) % 3]
        result.append(jnp.stack([first_edge[1] * second[2] - first_edge[2] * second[1], first_edge[2] * second[0] - first_edge[0] * second[2], first_edge[0] * second[1] - first_edge[1] * second[0]]))
    return result

def euler_flux(values):
    density = values[0]
    momentum = values[1:4]
    energy = values[4]
    velocity = momentum / density
    pressure = (GAMMA - 1.0) * (energy - 0.5 * lax.optimization_barrier(jnp.sum(momentum * velocity, axis=0)))
    fluxes = []
    for i in range(3):
        components = [momentum[i]]
        for m in range(3):
            component = momentum[m] * velocity[i]
            if m == i:
                component = component + pressure
            components.append(component)
        components.append((energy + pressure) * velocity[i])
        fluxes.append(jnp.stack(components))
    return (fluxes, velocity, pressure)

def numerical_flux(inner_face, outer_face, normal):
    inner_fluxes, inner_velocity, inner_pressure = euler_flux(inner_face)
    outer_fluxes, outer_velocity, outer_pressure = euler_flux(outer_face)
    inner_normal = sum((normal[i] * inner_fluxes[i] for i in range(3)))
    outer_normal = sum((normal[i] * outer_fluxes[i] for i in range(3)))
    area_square = lax.optimization_barrier(jnp.sum(normal * normal, axis=0))
    area_size = jnp.sqrt(area_square)
    inner_along = lax.optimization_barrier(jnp.sum(inner_velocity * normal, axis=0))
    outer_along = lax.optimization_barrier(jnp.sum(outer_velocity * normal, axis=0))
    inner_speed = jnp.sqrt(inner_along * inner_along + SOFTENING * area_square) + jnp.sqrt(GAMMA * inner_pressure / inner_face[0]) * area_size
    outer_speed = jnp.sqrt(outer_along * outer_along + SOFTENING * area_square) + jnp.sqrt(GAMMA * outer_pressure / outer_face[0]) * area_size
    difference = inner_speed - outer_speed
    wave_speed = 0.5 * (inner_speed + outer_speed) + 0.5 * jnp.sqrt(difference * difference + SOFTENING * area_square)
    common = 0.5 * (inner_normal + outer_normal) - 0.5 * wave_speed * (outer_face - inner_face)
    return common - inner_normal

def element_residual(values, neighbours, corners):
    points, weights, derivative = lobatto_tables()
    derivative = jnp.asarray(derivative, jnp.float32)
    volume_weights = jnp.asarray(weights[:, None, None] * weights[None, :, None] * weights[None, None, :], jnp.float32)
    face_weights = jnp.asarray(weights[:, None] * weights[None, :], jnp.float32).reshape(1, 16, 1)
    columns = values.shape[-1]
    normals = area_vectors(corners)
    fluxes = euler_flux(values)[0]
    patterns = ['ab,vbcde->vacde', 'ab,vcbde->vcade', 'ab,vcdbe->vcdae']
    divergence = jnp.zeros((5, 4, 4, 4, columns), jnp.float32)
    for j in range(3):
        contravariant = sum((normals[j][i] * fluxes[i] for i in range(3))).reshape(5, 4, 4, 4, columns)
        divergence = divergence + jnp.einsum(patterns[j], derivative, contravariant, precision=HIGHEST)
    result = divergence * volume_weights[None, :, :, :, None]
    reshaped = values.reshape(5, 4, 4, 4, columns)
    for f in range(6):
        j = f // 2
        face_side = f % 2
        inner_face = lax.index_in_dim(reshaped, 3 * face_side, axis=1 + j, keepdims=False).reshape(5, 16, columns)
        normal = lax.index_in_dim(normals[j].reshape(3, 4, 4, 4, columns), 3 * face_side, axis=1 + j, keepdims=False).reshape(3, 16, columns) * (2.0 * face_side - 1.0)
        jump_term = numerical_flux(inner_face, neighbours[f], normal) * face_weights
        location = (slice(None),) * (1 + j) + (3 * face_side,)
        result = result.at[location].add(jump_term.reshape(5, 4, 4, columns))
    return result.reshape(5, 64, columns)

def face_traces(values):
    columns = values.shape[-1]
    reshaped = values.reshape(5, 4, 4, 4, columns)
    return [lax.index_in_dim(reshaped, 3 * (f % 2), axis=1 + f // 2, keepdims=False).reshape(5, 16, columns) for f in range(6)]

def neighbour_states(traces, lower_halo, upper_halo, far_field, face_neighbour):
    outer_cell = jnp.broadcast_to(far_field.reshape(5, 1, 1), (5, 16, 1))
    empty_block = jnp.zeros_like(lower_halo)
    result = []
    for f in range(6):
        halo_part = lower_halo if f == 0 else upper_halo if f == 1 else empty_block
        lookup_table = jnp.concatenate([traces[f ^ 1], halo_part, outer_cell], axis=2)
        result.append(jnp.take(lookup_table, face_neighbour[f], axis=2))
    return result

def partition_major(array, partitions):
    array_shape = array.shape
    return jnp.moveaxis(array.reshape(array_shape[:-1] + (partitions, array_shape[-1] // partitions)), -2, 0)

def partition_minor(array):
    return jnp.moveaxis(array, 0, -2).reshape(array.shape[1:-1] + (-1,))

def reference(flow_state, state_tangent, far_field, coordinates, damping, face_neighbour, element_nodes, upper_sends, lower_sends, node_sends, shock_flags):
    partitions = N_PARTS
    states = partition_major(flow_state, partitions)
    tangents = partition_major(state_tangent, partitions)
    neighbour_lists = partition_major(face_neighbour, partitions)
    corner_lists = partition_major(element_nodes, partitions)
    upper_lists = partition_major(upper_sends, partitions)
    lower_lists = partition_major(lower_sends, partitions)
    node_lists = partition_major(node_sends, partitions)
    flag_rows = partition_major(shock_flags, partitions)
    places = partition_major(coordinates, partitions)
    strength = damping[0]
    smoothing = damping[1]
    laplacian = jnp.asarray(edge_laplacian(), jnp.float32)
    node_count = places.shape[2]
    halo_count = node_lists.shape[1]

    def outgoing(items):
        values, tangent, upper_list, lower_list, node_list, place = items
        traces = face_traces(values)
        tangent_traces = face_traces(tangent)
        return (jnp.take(traces[1], upper_list, axis=2), jnp.take(tangent_traces[1], upper_list, axis=2), jnp.take(traces[0], lower_list, axis=2), jnp.take(tangent_traces[0], lower_list, axis=2), jnp.take(place, node_list, axis=1))
    sent = lax.map(outgoing, (states, tangents, upper_lists, lower_lists, node_lists, places))
    lower_halos = jnp.roll(sent[0], 1, axis=0)
    lower_tangents = jnp.roll(sent[1], 1, axis=0)
    upper_halos = jnp.roll(sent[2], -1, axis=0)
    upper_tangents = jnp.roll(sent[3], -1, axis=0)
    halo_places = jnp.roll(sent[4], -1, axis=0)

    def first_pass(items):
        values, tangent, lower_halo, lower_tangent, upper_halo, upper_tangent, neighbour_list, corner_list, place, halo_place, flag_row = items
        outer_states = neighbour_states(face_traces(values), lower_halo, upper_halo, far_field, neighbour_list)
        outer_tangents = neighbour_states(face_traces(tangent), lower_tangent, upper_tangent, jnp.zeros_like(far_field), neighbour_list)
        corners = jnp.take(jnp.concatenate([place, halo_place], axis=1), corner_list, axis=1)
        residual, change = jax.jvp(lambda v, o: element_residual(v, o, corners), (values, outer_states), (tangent, outer_tangents))
        weight = flag_row.astype(jnp.float32)
        pullback = jax.vjp(lambda c: element_residual(values, outer_states, c), corners)[1]
        corner_grad = pullback(residual * weight)[0]
        corner_grad = corner_grad + smoothing * weight * jnp.einsum('ike,kl->ile', corners, laplacian, precision=HIGHEST)
        grad_table = jnp.zeros((3, node_count + halo_count), jnp.float32).at[:, corner_list].add(corner_grad)
        count_table = jnp.zeros((node_count + halo_count,), jnp.float32).at[corner_list].add(jnp.broadcast_to(weight, corner_list.shape))
        return (residual, change, grad_table, count_table)
    residuals, changes, grad_tables, count_tables = lax.map(first_pass, (states, tangents, lower_halos, lower_tangents, upper_halos, upper_tangents, neighbour_lists, corner_lists, places, halo_places, flag_rows))
    back_grads = jnp.roll(grad_tables[:, :, node_count:], 1, axis=0)
    back_counts = jnp.roll(count_tables[:, node_count:], 1, axis=0)

    def assemble(items):
        grad_table, count_table, node_list, back_grad, back_count = items
        gradient = grad_table[:, :node_count].at[:, node_list].add(back_grad)
        touched = count_table[:node_count].at[node_list].add(back_count)
        return -jnp.where(touched > 0.5, gradient, 0.0)
    descents = lax.map(assemble, (grad_tables, count_tables, node_lists, back_grads, back_counts))
    halo_descents = jnp.roll(jnp.take_along_axis(descents, node_lists[:, None, :], axis=2), -1, axis=0)

    def second_pass(items):
        values, lower_halo, upper_halo, neighbour_list, corner_list, place, halo_place, descent, halo_descent, flag_row = items
        outer_states = neighbour_states(face_traces(values), lower_halo, upper_halo, far_field, neighbour_list)
        corners = jnp.take(jnp.concatenate([place, halo_place], axis=1), corner_list, axis=1)
        corner_step = jnp.take(jnp.concatenate([descent, halo_descent], axis=1), corner_list, axis=1)
        change = jax.jvp(lambda c: element_residual(values, outer_states, c), (corners,), (corner_step,))[1]
        weight = flag_row.astype(jnp.float32)
        curvature = jnp.sum(weight * change * change)
        bending = smoothing * jnp.sum(weight * lax.optimization_barrier(jnp.sum(corner_step * jnp.einsum('ike,kl->ile', corner_step, laplacian, precision=HIGHEST), axis=(0, 1))))
        return (curvature, bending)
    curvatures, bendings = lax.map(second_pass, (states, lower_halos, upper_halos, neighbour_lists, corner_lists, places, halo_places, descents, halo_descents, flag_rows))
    norm_total = jnp.sum(descents * descents)
    step_size = norm_total / (jnp.sum(curvatures) + jnp.sum(bendings) + strength * norm_total)
    return (partition_minor(residuals), partition_minor(changes), partition_minor(step_size * descents))
```

```python
import functools
import math

import jax
import jax.numpy as jnp
import numpy as np
from jax import lax
from jax.experimental import pallas as pl
from jax.experimental.pallas import tpu as pltpu
from jax.sharding import PartitionSpec as P

GAMMA = 1.4
SOFTENING = 0.01
HIGHEST = lax.Precision.HIGHEST
F32 = jnp.float32


def lobatto_tables():
    points = np.array([-1.0, -math.sqrt(0.2), math.sqrt(0.2), 1.0])
    weights = np.array([1.0, 5.0, 5.0, 1.0]) / 6.0
    derivative = np.zeros((4, 4))
    for a in range(4):
        for b in range(4):
            if a == b:
                derivative[a, b] = sum((1.0 / (points[a] - points[m]) for m in range(4) if m != a))
            else:
                numerator = 1.0
                denominator = 1.0
                for m in range(4):
                    if m != b:
                        denominator *= points[b] - points[m]
                        if m != a:
                            numerator *= points[a] - points[m]
                derivative[a, b] = numerator / denominator
    return (points, weights, derivative)


def shape_gradients():
    points = lobatto_tables()[0]
    gradients = np.zeros((3, 64, 8))
    for q in range(64):
        position = (q // 16, q // 4 % 4, q % 4)
        for k in range(8):
            corner_bits = (k // 4, k // 2 % 2, k % 2)
            for j in range(3):
                factor = 1.0
                for m in range(3):
                    orient = 1.0 if corner_bits[m] == 1 else -1.0
                    if m == j:
                        factor *= 0.5 * orient
                    else:
                        factor *= 0.5 * (1.0 + orient * points[position[m]])
                gradients[j, q, k] = factor
    return gradients


def edge_laplacian():
    matrix = np.zeros((8, 8))
    for k in range(8):
        matrix[k, k] = 3.0
        for b in range(3):
            matrix[k, k ^ 1 << b] = -1.0
    return matrix


def face_rows(j, s):
    rows = [q for q in range(64) if (q // 16, q // 4 % 4, q % 4)[j] == 3 * s]
    return np.array(rows)


def constant_matrices():
    points, weights, derivative = lobatto_tables()
    volume = np.einsum("a,b,c->abc", weights, weights, weights).reshape(64)
    face = np.einsum("a,b->ab", weights, weights).reshape(16)
    eye = np.eye(4)
    full = [
        np.kron(np.kron(derivative, eye), eye),
        np.kron(np.kron(eye, derivative), eye),
        np.kron(np.kron(eye, eye), derivative),
    ]
    assemble = np.zeros((128, 144))
    for half in range(2):
        rows = slice(64 * half, 64 * half + 64)
        for j in range(3):
            weighted = volume[:, None] * full[j]
            assemble[rows, 32 * j : 32 * j + 32] = weighted[:, 32 * half : 32 * half + 32]
            for point, q in enumerate(face_rows(j, half)):
                assemble[64 * half + q, 96 + 16 * j + point] = face[point]
    gradients = shape_gradients()
    corner = np.zeros((200, 16))
    for half in range(2):
        columns = slice(8 * half, 8 * half + 8)
        for j in range(3):
            corner[32 * j : 32 * j + 32, columns] = gradients[j, 32 * half : 32 * half + 32]
            for which in range(2):
                base = 96 + 48 * which + 16 * j
                corner[base : base + 16, columns] = gradients[(j + 1 + which) % 3][
                    face_rows(j, half)
                ]
    corner[192:200, 0:8] = edge_laplacian()
    return assemble.astype(np.float32), corner.astype(np.float32)


def dot(a, b):
    return jnp.dot(a, b, precision=HIGHEST, preferred_element_type=F32)


def dot_transposed(a, b):
    return lax.dot_general(
        a, b, (((1,), (1,)), ((), ())), precision=HIGHEST, preferred_element_type=F32
    )


def lanes(rows=8):
    return lax.broadcasted_iota(jnp.int32, (rows, 128), 1)


def pair(left, right):
    return jnp.concatenate([left, right], axis=1)


def pick(table, index):
    blocks = [
        jnp.take_along_axis(table[r : r + 8], index, axis=1, mode="promise_in_bounds")
        for r in range(0, table.shape[0], 8)
    ]
    return blocks[0] if len(blocks) == 1 else jnp.concatenate(blocks, axis=0)


def spread(row, rows=8):
    return jnp.broadcast_to(row, (rows, row.shape[1]))


def pad_lanes(value, width=128):
    fill = jnp.zeros((value.shape[0], width - value.shape[1]), value.dtype)
    return jnp.concatenate([value, fill], axis=1)


def primitives(values):
    density = values[0]
    momentum = values[1:4]
    energy = values[4]
    inverse = 1.0 / density
    velocity = [m * inverse for m in momentum]
    kinetic = sum(m * v for m, v in zip(momentum, velocity))
    pressure = (GAMMA - 1.0) * (energy - 0.5 * kinetic)
    return (density, velocity, pressure, momentum, energy + pressure, inverse)


def along_flux(prims, normal):
    density, velocity, pressure, momentum, total, _ = prims
    along = sum(v * n for v, n in zip(velocity, normal))
    return (
        [density * along]
        + [m * along + pressure * n for m, n in zip(momentum, normal)]
        + [total * along]
    )


def along_flux_transposed(prims, cotangent):
    density, velocity, pressure, momentum, total, _ = prims
    scale = density * cotangent[0] + total * cotangent[4]
    for m in range(3):
        scale = scale + momentum[m] * cotangent[1 + m]
    return [velocity[i] * scale + pressure * cotangent[1 + i] for i in range(3)]


def cross(a, b):
    return [
        a[1] * b[2] - a[2] * b[1],
        a[2] * b[0] - a[0] * b[2],
        a[0] * b[1] - a[1] * b[0],
    ]


def added(a, b):
    return [x + y for x, y in zip(a, b)]


def signal_speed(prims, normal, area_square, area):
    density, velocity, pressure, _, _, inverse = prims
    along = sum(v * n for v, n in zip(velocity, normal))
    root = jnp.sqrt(along * along + SOFTENING * area_square)
    sound = jnp.sqrt(GAMMA * pressure * inverse)
    return root + sound * area, along, root, sound


def jump_of(inner, outer, normal, area_square, area):
    inner_prims = primitives(inner)
    outer_prims = primitives(outer)
    inner_speed = signal_speed(inner_prims, normal, area_square, area)[0]
    outer_speed = signal_speed(outer_prims, normal, area_square, area)[0]
    difference = inner_speed - outer_speed
    wave = 0.5 * (inner_speed + outer_speed) + 0.5 * jnp.sqrt(
        difference * difference + SOFTENING * area_square
    )
    inner_flux = along_flux(inner_prims, normal)
    outer_flux = along_flux(outer_prims, normal)
    return [
        0.5 * (outer_flux[v] - inner_flux[v]) - 0.5 * wave * (outer[v] - inner[v])
        for v in range(5)
    ]


def wave_gradient(inner_prims, outer_prims, normal, area_square, area):
    inner_speed, along_u, root_u, sound_u = signal_speed(inner_prims, normal, area_square, area)
    outer_speed, along_w, root_w, sound_w = signal_speed(outer_prims, normal, area_square, area)
    difference = inner_speed - outer_speed
    spread_root = jnp.sqrt(difference * difference + SOFTENING * area_square)
    over_u = 1.0 / root_u
    over_w = 1.0 / root_w
    over_area = 1.0 / area
    over_spread = 0.5 / spread_root
    result = []
    for i in range(3):
        slope_u = (along_u * inner_prims[1][i] + SOFTENING * normal[i]) * over_u + (
            sound_u * over_area
        ) * normal[i]
        slope_w = (along_w * outer_prims[1][i] + SOFTENING * normal[i]) * over_w + (
            sound_w * over_area
        ) * normal[i]
        result.append(
            0.5 * (slope_u + slope_w)
            + (difference * (slope_u - slope_w) + SOFTENING * normal[i]) * over_spread
        )
    return result


def pack_kernel(
    odd_ref, flow_ref, tangent_ref, places_ref, upper_ref, lower_ref, nodes_ref, a_ref, b_ref
):
    odd = odd_ref[0] == 1
    lane = lanes()
    group = lane // 32

    def faces(list_ref, row):
        index = pad_lanes(list_ref[...])
        index = spread(index)
        tiled = index
        for g in range(1, 4):
            tiled = jnp.where(group == g, pltpu.roll(index, 32 * g, 1), tiled)
        chunks = []
        for first in range(0, 12, 4):
            merged = None
            for g in range(4):
                v = first + g
                if v >= 10:
                    continue
                source = flow_ref if v < 5 else tangent_ref
                block = pad_lanes(source[v % 5, row : row + 16, :])
                block = pick(block, tiled)
                own = jnp.concatenate([group, group], axis=0) == g
                merged = jnp.where(own, block, 0.0 if merged is None else merged)
            chunks.append(merged)
        return jnp.concatenate(chunks, axis=0)

    up = faces(upper_ref, 48)
    down = faces(lower_ref, 0)
    node_index = spread(pad_lanes(nodes_ref[...]))
    places = jnp.concatenate([places_ref[...], jnp.zeros((5, 102), F32)], axis=0)
    nodes = pick(pad_lanes(places), node_index)
    none = jnp.zeros((8, 128), F32)
    up = jnp.concatenate([up, none], axis=0)
    down = jnp.concatenate([down, nodes], axis=0)
    a_ref[...] = jnp.where(odd, down, up)
    b_ref[...] = jnp.where(odd, up, down)


def face_pairs(ref, v):
    value = ref[v]
    sides = []
    for s in range(2):
        first = value[48 * s : 48 * s + 16]
        second = jnp.concatenate(
            [value[16 * i + 12 * s : 16 * i + 12 * s + 4] for i in range(4)], axis=0
        )
        third = ref[pl.ds(v, 1), pl.ds(3 * s, 16, stride=4), :][0]
        sides.append(jnp.concatenate([first, second, third], axis=0))
    return pair(sides[0], sides[1])


def volume_pairs(ref, v):
    return pair(ref[v, 0:32, :], ref[v, 32:64, :])


def corner_values(index, own_rows, halo_rows):
    local = index < 102
    own_index = jnp.where(local, index, 0)
    halo_index = jnp.where(local, 0, index - 102)
    result = []
    for i in range(3):
        own = pick(spread(own_rows[i : i + 1]), own_index)
        halo = pick(spread(halo_rows[i : i + 1]), halo_index)
        result.append(jnp.where(local, own, halo))
    return result


def corner_operand(values):
    low = lanes() < 64
    blocks = [
        jnp.concatenate([jnp.where(low, v, 0.0), jnp.where(low, 0.0, v)], axis=0) for v in values
    ]
    return jnp.concatenate(blocks, axis=1)


def columns(array, rows, i):
    return array[rows, 128 * i : 128 * i + 128]


def tangents_of(spans):
    volume = [[columns(spans, slice(32 * j, 32 * j + 32), i) for i in range(3)] for j in range(3)]
    faces = [
        [columns(spans, slice(96 + 48 * w, 144 + 48 * w), i) for i in range(3)] for w in range(2)
    ]
    return volume, faces


def folded(product, v):
    block = product[:, 128 * v : 128 * v + 128]
    return block[0:64] + pltpu.roll(block[64:128], 64, 1)


def side_sign():
    return jnp.where(lanes(48) < 64, -1.0, 1.0).astype(F32)


def main_kernel(
    odd_ref,
    far_ref,
    damping_ref,
    flow_ref,
    tangent_ref,
    places_ref,
    neighbour_ref,
    nodes_ref,
    sends_ref,
    flags_ref,
    a_ref,
    b_ref,
    assemble_ref,
    transposed_ref,
    corner_ref,
    corner_transposed_ref,
    residual_ref,
    change_ref,
    table_ref,
    send_a_ref,
    send_b_ref,
    spans_ref,
    outer_ref,
    slopes_ref,
    joined_ref,
):
    odd = odd_ref[0] == 1
    lane = lanes()
    low = lane < 64
    low16 = lanes(16) < 64
    from_a = a_ref[...]
    from_b = b_ref[...]
    lower = jnp.where(odd, from_a, from_b)
    upper = jnp.where(odd, from_b, from_a)

    node_index = pair(nodes_ref[...], nodes_ref[...])
    places = pad_lanes(places_ref[...])
    corners = corner_values(node_index, places, upper[48:56])
    relative = [c - c[0:1] for c in corners]
    spans = dot(corner_ref[...], corner_operand(relative))
    spans_ref[...] = spans
    volume_spans, face_spans = tangents_of(spans)
    normals = [cross(volume_spans[(j + 1) % 3], volume_spans[(j + 2) % 3]) for j in range(3)]
    sign = side_sign()
    face_normal = [sign * n for n in cross(face_spans[0], face_spans[1])]
    area_square = sum(n * n for n in face_normal)
    area = jnp.sqrt(area_square)

    inner = [face_pairs(flow_ref, v) for v in range(5)]
    inner_change = [face_pairs(tangent_ref, v) for v in range(5)]
    neighbours = neighbour_ref[...]
    listed = [
        spread(pair(neighbours[2 * j : 2 * j + 1], neighbours[2 * j + 1 : 2 * j + 2]))
        for j in range(3)
    ]
    gather_index = []
    for j in range(3):
        local = jnp.where(listed[j] < 64, listed[j], 0)
        gather_index.append(jnp.where(low, local + 64, local))
    slot = jnp.clip(listed[0] - 64, 0, 31)
    far16 = [jnp.concatenate([m, m], axis=0) == 96 for m in listed]
    halo16 = jnp.concatenate([listed[0], listed[0]], axis=0) >= 64

    def outside(face_values, v, far_value):
        rows = []
        for j in range(3):
            block = pick(face_values[16 * j : 16 * j + 16], gather_index[j])
            if j == 0:
                base, g = 16 * (v // 4), v % 4
                shifted_slot = slot + 32 * g
                below = pick(lower[base : base + 16], shifted_slot)
                above = pick(upper[base : base + 16], shifted_slot)
                block = jnp.where(halo16, jnp.where(low16, below, above), block)
            rows.append(jnp.where(far16[j], far_value, block))
        return jnp.concatenate(rows, axis=0)

    outer = [outside(inner[v], v, far_ref[v]) for v in range(5)]
    outer_change = [outside(inner_change[v], 5 + v, 0.0) for v in range(5)]
    for v in range(5):
        outer_ref[v] = outer[v]

    jump, jump_change = jax.jvp(
        lambda u, w: jump_of(u, w, face_normal, area_square, area),
        (inner, outer),
        (inner_change, outer_change),
    )
    state = [volume_pairs(flow_ref, v) for v in range(5)]
    state_change = [volume_pairs(tangent_ref, v) for v in range(5)]

    def volume_flux(u):
        prims = primitives(u)
        return [along_flux(prims, normals[j]) for j in range(3)]

    fluxes, flux_changes = jax.jvp(volume_flux, (state,), (state_change,))
    stacked = [
        jnp.concatenate([fluxes[0][v], fluxes[1][v], fluxes[2][v], jump[v]], axis=0)
        for v in range(5)
    ] + [
        jnp.concatenate(
            [flux_changes[0][v], flux_changes[1][v], flux_changes[2][v], jump_change[v]], axis=0
        )
        for v in range(5)
    ]
    assemble = assemble_ref[...]
    product = dot(assemble, jnp.concatenate(stacked, axis=1))
    residual = [folded(product, v) for v in range(5)]
    for v in range(5):
        residual_ref[v] = residual[v][:, 0:64]
        change_ref[v] = folded(product, 5 + v)[:, 0:64]

    weight = flags_ref[...].astype(F32)
    weight = pair(weight, weight)
    low64 = lanes(64) < 64
    seeds = []
    for v in range(5):
        seed = residual[v] * weight
        seeds.append(
            jnp.concatenate(
                [jnp.where(low64, seed, 0.0), jnp.where(low64, 0.0, pltpu.roll(seed, 64, 1))],
                axis=0,
            )
        )
    back = dot(transposed_ref[...], jnp.concatenate(seeds, axis=1))
    prims = primitives(state)
    normal_bar = []
    for j in range(3):
        cotangent = [columns(back, slice(32 * j, 32 * j + 32), v) for v in range(5)]
        normal_bar.append(along_flux_transposed(prims, cotangent))
    cotangent = [columns(back, slice(96, 144), v) for v in range(5)]
    inner_prims = primitives(inner)
    outer_prims = primitives(outer)
    slopes = wave_gradient(inner_prims, outer_prims, face_normal, area_square, area)
    for i in range(3):
        slopes_ref[i] = slopes[i]
    lift = sum(c * (w - u) for c, w, u in zip(cotangent, outer, inner))
    from_outer = along_flux_transposed(outer_prims, cotangent)
    from_inner = along_flux_transposed(inner_prims, cotangent)
    face_bar = [
        (0.5 * sign) * (from_outer[i] - from_inner[i] - lift * slopes[i]) for i in range(3)
    ]
    span_bar = []
    for j in range(3):
        first = cross(volume_spans[(j + 1) % 3], normal_bar[(j + 2) % 3])
        second = cross(normal_bar[(j + 1) % 3], volume_spans[(j + 2) % 3])
        span_bar.append(added(first, second))
    face_span_bar = [cross(face_spans[1], face_bar), cross(face_bar, face_spans[0])]
    stacked_bar = jnp.concatenate(
        [
            jnp.concatenate(
                [span_bar[j][i] for j in range(3)] + [face_span_bar[w][i] for w in range(2)],
                axis=0,
            )
            for i in range(3)
        ],
        axis=1,
    )
    corner_bar = dot(corner_transposed_ref[...], stacked_bar)
    smoothing = damping_ref[1]
    pieces = []
    for i in range(3):
        block = columns(corner_bar, slice(0, 16), i)
        bar = block[0:8] + pltpu.roll(block[8:16], 64, 1)
        bar = bar + smoothing * weight * columns(spans, slice(192, 200), i)
        pieces.append(bar)
    pieces.append(spread(weight))
    gradient = jnp.concatenate(pieces, axis=0)
    gradient = jnp.where(lanes(32) < 64, gradient, pltpu.roll(gradient, 64, 1))
    row_corner = lax.broadcasted_iota(jnp.int32, (32, 128), 0) % 8
    half = jnp.where(lanes(32) < 64, 0, 1)
    left = []
    right = []
    node_row = lax.broadcasted_iota(jnp.int32, (256, 128), 0)
    node_row = jnp.where(node_row < 128, node_row, node_row - 26)
    for p in range(4):
        left.append(jnp.where(row_corner == 2 * p + half, gradient, 0.0))
        named = jnp.where(low[0:1], node_index[2 * p : 2 * p + 1], node_index[2 * p + 1 : 2 * p + 2])
        right.append((node_row == named).astype(F32))
    right = [
        jnp.where((node_row[:, :] < 102) | (lax.broadcasted_iota(jnp.int32, (256, 128), 0) >= 128), r, 0.0)
        for r in right
    ]
    scattered = dot_transposed(jnp.concatenate(left, axis=1), jnp.concatenate(right, axis=1))
    rows = [jnp.sum(scattered[8 * i : 8 * i + 8], axis=0, keepdims=True) for i in range(4)]
    table = jnp.concatenate(rows + [jnp.zeros((4, 256), F32)], axis=0)
    table_ref[...] = table
    send_index = spread(pad_lanes(sends_ref[...]))
    up = table[:, 128:256]
    down = jnp.where(lane < 51, pick(table[:, 0:128], send_index), 0.0)
    send_a_ref[...] = jnp.where(odd, down, up)
    send_b_ref[...] = jnp.where(odd, up, down)
    joined_ref[...] = jnp.zeros((8, 128), F32)


def second_kernel(
    odd_ref,
    damping_ref,
    flow_ref,
    nodes_ref,
    sends_ref,
    flags_ref,
    table_ref,
    a_ref,
    b_ref,
    spans_ref,
    outer_ref,
    slopes_ref,
    assemble_ref,
    corner_ref,
    descent_ref,
    sums_ref,
):
    odd = odd_ref[0] == 1
    lane = lanes()
    from_a = a_ref[...]
    from_b = b_ref[...]
    lower = jnp.where(odd, from_a, from_b)
    upper = jnp.where(odd, from_b, from_a)
    table = table_ref[...]
    send_row = jnp.where(lane[0:1] < 51, pad_lanes(sends_ref[...]), -1)
    chosen = (lax.broadcasted_iota(jnp.int32, (128, 128), 0) == send_row).astype(F32)
    own = table[:, 0:128] + dot_transposed(jnp.where(lane < 51, lower, 0.0), chosen)
    halo = table[:, 128:256] + upper
    own = -jnp.where(own[3:4] > 0.5, own, 0.0)
    halo = -jnp.where(halo[3:4] > 0.5, halo, 0.0)
    descent_ref[...] = own[0:3]
    moved = jnp.where(lax.broadcasted_iota(jnp.int32, (8, 128), 0) < 3, own, 0.0)
    norm = jnp.sum(moved * moved, axis=(0, 1), keepdims=True)

    node_index = pair(nodes_ref[...], nodes_ref[...])
    steps = corner_values(node_index, own, halo)
    moves = dot(corner_ref[...], corner_operand(steps))
    volume_moves, face_moves = tangents_of(moves)
    volume_spans, face_spans = tangents_of(spans_ref[...])
    state = primitives([volume_pairs(flow_ref, v) for v in range(5)])
    fluxes = []
    for j in range(3):
        a, b = (j + 1) % 3, (j + 2) % 3
        normal_move = added(
            cross(volume_moves[a], volume_spans[b]), cross(volume_spans[a], volume_moves[b])
        )
        fluxes.append(along_flux(state, normal_move))
    sign = side_sign()
    face_move = [
        sign * n
        for n in added(cross(face_moves[0], face_spans[1]), cross(face_spans[0], face_moves[1]))
    ]
    inner = [face_pairs(flow_ref, v) for v in range(5)]
    outer = [outer_ref[v] for v in range(5)]
    inner_flux = along_flux(primitives(inner), face_move)
    outer_flux = along_flux(primitives(outer), face_move)
    wave_move = sum(slopes_ref[i] * face_move[i] for i in range(3))
    jump = [
        0.5 * (outer_flux[v] - inner_flux[v] - wave_move * (outer[v] - inner[v]))
        for v in range(5)
    ]
    stacked = [
        jnp.concatenate([fluxes[0][v], fluxes[1][v], fluxes[2][v], jump[v]], axis=0)
        for v in range(5)
    ]
    product = dot(assemble_ref[...], jnp.concatenate(stacked, axis=1))
    square = None
    for v in range(5):
        change = folded(product, v)
        square = change * change if square is None else square + change * change
    weight = flags_ref[...].astype(F32)
    weight = pad_lanes(weight)
    curvature = jnp.sum(jnp.sum(square, axis=0, keepdims=True) * weight, axis=1, keepdims=True)
    bend = sum(steps[i] * columns(moves, slice(192, 200), i) for i in range(3))
    bending = damping_ref[1] * jnp.sum(
        jnp.sum(bend, axis=0, keepdims=True) * weight, axis=1, keepdims=True
    )
    sums_ref[...] = jnp.where(
        lane[0:1] == 0, norm, jnp.where(lane[0:1] == 1, curvature + bending, 0.0)
    )


def call(kernel, out_shape, smem, arrays):
    scalar = pl.BlockSpec(memory_space=pltpu.SMEM)
    vector = pl.BlockSpec(memory_space=pltpu.VMEM)
    return pl.pallas_call(
        kernel,
        out_shape=[jax.ShapeDtypeStruct(s, F32) for s in out_shape],
        in_specs=[scalar] * smem + [vector] * (len(arrays) - smem),
        out_specs=[vector] * len(out_shape),
        name=kernel.__name__,
    )(*arrays)


def exchange(value_a, value_b, count):
    b = lax.ppermute(
        value_b,
        "parts",
        [(i, (i - 1) % count if i % 2 == 0 else (i + 1) % count) for i in range(count)],
    )
    a = lax.ppermute(value_a, "parts", [(i, i ^ 1) for i in range(count)])
    return a, b


def summed(row, count):
    inner = min(16, count)
    near = [[base + g for g in range(inner)] for base in range(0, count, inner)]
    far = [[base + inner * g for g in range(count // inner)] for base in range(inner)]
    for groups in (near, far):
        size = len(groups[0])
        if size > 1:
            sent = jnp.broadcast_to(row[None], (size,) + row.shape)
            row = jnp.sum(
                lax.all_to_all(sent, "parts", 0, 0, axis_index_groups=groups), axis=0
            )
    return row


def body(
    flow_state,
    state_tangent,
    far_field,
    coordinates,
    damping,
    face_neighbour,
    element_nodes,
    upper_sends,
    lower_sends,
    node_sends,
    shock_flags,
):
    count = lax.axis_size("parts")
    assemble, corner = constant_matrices()
    odd = (lax.axis_index("parts") % 2).astype(jnp.int32).reshape(1)
    sends_row = node_sends.reshape(1, 51)
    flags_row = shock_flags.reshape(1, 64)
    pack_a, pack_b = call(
        pack_kernel,
        [(56, 128)] * 2,
        1,
        (
            odd,
            flow_state,
            state_tangent,
            coordinates,
            upper_sends.reshape(1, 32),
            lower_sends.reshape(1, 32),
            sends_row,
        ),
    )
    got_a, got_b = exchange(pack_a, pack_b, count)
    residual, change, table, send_a, send_b, spans, outer, slopes, _ = call(
        main_kernel,
        [
            (5, 64, 64),
            (5, 64, 64),
            (8, 256),
            (8, 128),
            (8, 128),
            (200, 384),
            (5, 48, 128),
            (3, 48, 128),
            (8, 128),
        ],
        3,
        (
            odd,
            far_field,
            damping,
            flow_state,
            state_tangent,
            coordinates,
            face_neighbour,
            element_nodes,
            sends_row,
            flags_row,
            got_a,
            got_b,
            jnp.asarray(assemble),
            jnp.asarray(assemble.T.copy()),
            jnp.asarray(corner),
            jnp.asarray(corner[:192].T.copy()),
        ),
    )
    back_a, back_b = exchange(send_a, send_b, count)
    descent, sums = call(
        second_kernel,
        [(3, 128), (1, 128)],
        2,
        (
            odd,
            damping,
            flow_state,
            element_nodes,
            sends_row,
            flags_row,
            table,
            back_a,
            back_b,
            spans,
            outer,
            slopes,
            jnp.asarray(assemble),
            jnp.asarray(corner),
        ),
    )
    total = summed(sums[0], count)
    step = total[0] / (total[1] + damping[0] * total[0])
    return (residual, change, step * descent[:, 0:102])


def solution(mesh):
    in_specs = (
        P(None, None, "parts"),
        P(None, None, "parts"),
        P(),
        P(None, "parts"),
        P(),
        P(None, "parts"),
        P(None, "parts"),
        P("parts"),
        P("parts"),
        P("parts"),
        P("parts"),
    )
    out_specs = (P(None, None, "parts"), P(None, None, "parts"), P(None, "parts"))
    return jax.shard_map(body, mesh=mesh, in_specs=in_specs, out_specs=out_specs, check_vma=False)
```

```python
import math

import jax
import jax.numpy as jnp
import numpy as np
from jax import lax
from jax.experimental import pallas as pl
from jax.experimental.pallas import tpu as pltpu
from jax.sharding import PartitionSpec as P


GAMMA = 1.4
SOFTENING = 0.01
HIGHEST = lax.Precision.HIGHEST
F32 = jnp.float32


def lobatto_tables():
    points = np.array([-1.0, -math.sqrt(0.2), math.sqrt(0.2), 1.0])
    weights = np.array([1.0, 5.0, 5.0, 1.0]) / 6.0
    derivative = np.zeros((4, 4))
    for a in range(4):
        for b in range(4):
            if a == b:
                derivative[a, b] = sum((1.0 / (points[a] - points[m]) for m in range(4) if m != a))
            else:
                numerator = 1.0
                denominator = 1.0
                for m in range(4):
                    if m != b:
                        denominator *= points[b] - points[m]
                        if m != a:
                            numerator *= points[a] - points[m]
                derivative[a, b] = numerator / denominator
    return (points, weights, derivative)


def shape_gradients():
    points = lobatto_tables()[0]
    gradients = np.zeros((3, 64, 8))
    for q in range(64):
        position = (q // 16, q // 4 % 4, q % 4)
        for k in range(8):
            corner_bits = (k // 4, k // 2 % 2, k % 2)
            for j in range(3):
                factor = 1.0
                for m in range(3):
                    orient = 1.0 if corner_bits[m] == 1 else -1.0
                    if m == j:
                        factor *= 0.5 * orient
                    else:
                        factor *= 0.5 * (1.0 + orient * points[position[m]])
                gradients[j, q, k] = factor
    return gradients


def edge_laplacian():
    matrix = np.zeros((8, 8))
    for k in range(8):
        matrix[k, k] = 3.0
        for b in range(3):
            matrix[k, k ^ 1 << b] = -1.0
    return matrix


def face_rows(j, s):
    rows = [q for q in range(64) if (q // 16, q // 4 % 4, q % 4)[j] == 3 * s]
    return np.array(rows)


def constant_matrices():
    _, weights, derivative = lobatto_tables()
    volume = np.einsum("a,b,c->abc", weights, weights, weights).reshape(64)
    face = np.einsum("a,b->ab", weights, weights).reshape(16)
    eye = np.eye(4)
    full = [
        np.kron(np.kron(derivative, eye), eye),
        np.kron(np.kron(eye, derivative), eye),
        np.kron(np.kron(eye, eye), derivative),
    ]
    assemble = np.zeros((128, 144))
    for half in range(2):
        rows = slice(64 * half, 64 * half + 64)
        for j in range(3):
            weighted = volume[:, None] * full[j]
            assemble[rows, 32 * j : 32 * j + 32] = weighted[:, 32 * half : 32 * half + 32]
            for point, q in enumerate(face_rows(j, half)):
                assemble[64 * half + q, 96 + 16 * j + point] = face[point]
    gradients = shape_gradients()
    corner = np.zeros((200, 16))
    for half in range(2):
        columns = slice(8 * half, 8 * half + 8)
        for j in range(3):
            corner[32 * j : 32 * j + 32, columns] = gradients[j, 32 * half : 32 * half + 32]
            for which in range(2):
                base = 96 + 48 * which + 16 * j
                corner[base : base + 16, columns] = gradients[(j + 1 + which) % 3][
                    face_rows(j, half)
                ]
    corner[192:200, 0:8] = edge_laplacian()
    return assemble.astype(np.float32), corner.astype(np.float32)


def constant_tables():
    assemble, corner = constant_matrices()
    tables = np.zeros((488, 256), np.float32)
    tables[0:128, 0:144] = assemble
    tables[128:272, 0:128] = assemble.T
    tables[272:472, 0:16] = corner
    tables[472:488, 0:192] = corner[0:192].T
    return tables


def dot(a, b):
    return jnp.dot(a, b, precision=HIGHEST, preferred_element_type=F32)


def placed(a, chosen):
    rows = a.shape[0]
    parts = []
    for _ in range(3):
        part = a.astype(jnp.bfloat16)
        parts.append(part)
        a = a - part.astype(F32)
    product = lax.dot_general(
        jnp.concatenate(parts, axis=0),
        chosen,
        (((1,), (1,)), ((), ())),
        preferred_element_type=F32,
    )
    return product[0:rows] + product[rows : 2 * rows] + product[2 * rows : 3 * rows]


def lanes(rows=8):
    return lax.broadcasted_iota(jnp.int32, (rows, 128), 1)


def pair(left, right):
    return jnp.concatenate([left, right], axis=1)


def pick(table, index):
    blocks = [
        jnp.take_along_axis(table[r : r + 8], index, axis=1, mode="promise_in_bounds")
        for r in range(0, table.shape[0], 8)
    ]
    return blocks[0] if len(blocks) == 1 else jnp.concatenate(blocks, axis=0)


def spread(row, rows=8):
    return jnp.broadcast_to(row, (rows, row.shape[1]))


def pad_lanes(value, width=128):
    fill = jnp.zeros((value.shape[0], width - value.shape[1]), value.dtype)
    return jnp.concatenate([value, fill], axis=1)


def primitives(values):
    density = values[0]
    momentum = values[1:4]
    energy = values[4]
    inverse = 1.0 / density
    velocity = [m * inverse for m in momentum]
    kinetic = sum(m * v for m, v in zip(momentum, velocity))
    pressure = (GAMMA - 1.0) * (energy - 0.5 * kinetic)
    return (density, velocity, pressure, momentum, energy + pressure, inverse)


def along_flux(prims, normal):
    density, velocity, pressure, momentum, total, _ = prims
    along = sum(v * n for v, n in zip(velocity, normal))
    return (
        [density * along]
        + [m * along + pressure * n for m, n in zip(momentum, normal)]
        + [total * along]
    )


def along_flux_transposed(prims, cotangent):
    density, velocity, pressure, momentum, total, _ = prims
    scale = density * cotangent[0] + total * cotangent[4]
    for m in range(3):
        scale = scale + momentum[m] * cotangent[1 + m]
    return [velocity[i] * scale + pressure * cotangent[1 + i] for i in range(3)]


def cross(a, b):
    return [
        a[1] * b[2] - a[2] * b[1],
        a[2] * b[0] - a[0] * b[2],
        a[0] * b[1] - a[1] * b[0],
    ]


def added(a, b):
    return [x + y for x, y in zip(a, b)]


def signal_speed(prims, normal, area_square, area):
    _, velocity, pressure, _, _, inverse = prims
    along = sum(v * n for v, n in zip(velocity, normal))
    root = jnp.sqrt(along * along + SOFTENING * area_square)
    sound = jnp.sqrt(GAMMA * pressure * inverse)
    return root + sound * area, along, root, sound


def jump_of(inner, outer, normal, area_square, area):
    inner_prims = primitives(inner)
    outer_prims = primitives(outer)
    inner_speed = signal_speed(inner_prims, normal, area_square, area)[0]
    outer_speed = signal_speed(outer_prims, normal, area_square, area)[0]
    difference = inner_speed - outer_speed
    wave = 0.5 * (inner_speed + outer_speed) + 0.5 * jnp.sqrt(
        difference * difference + SOFTENING * area_square
    )
    inner_flux = along_flux(inner_prims, normal)
    outer_flux = along_flux(outer_prims, normal)
    return [
        0.5 * (outer_flux[v] - inner_flux[v]) - 0.5 * wave * (outer[v] - inner[v])
        for v in range(5)
    ]


def wave_gradient(inner_prims, outer_prims, normal, area_square, area):
    inner_speed, along_u, root_u, sound_u = signal_speed(inner_prims, normal, area_square, area)
    outer_speed, along_w, root_w, sound_w = signal_speed(outer_prims, normal, area_square, area)
    difference = inner_speed - outer_speed
    spread_root = jnp.sqrt(difference * difference + SOFTENING * area_square)
    over_u = 1.0 / root_u
    over_w = 1.0 / root_w
    over_area = 1.0 / area
    over_spread = 0.5 / spread_root
    result = []
    for i in range(3):
        slope_u = (along_u * inner_prims[1][i] + SOFTENING * normal[i]) * over_u + (
            sound_u * over_area
        ) * normal[i]
        slope_w = (along_w * outer_prims[1][i] + SOFTENING * normal[i]) * over_w + (
            sound_w * over_area
        ) * normal[i]
        result.append(
            0.5 * (slope_u + slope_w)
            + (difference * (slope_u - slope_w) + SOFTENING * normal[i]) * over_spread
        )
    return result


def on_odd():
    return (lax.axis_index("parts") & 1) == 1


def pack_kernel(
    flow_hbm,
    tangent_hbm,
    places_hbm,
    upper_hbm,
    lower_hbm,
    nodes_hbm,
    a_ref,
    b_ref,
    flow_ref,
    tangent_ref,
    places_ref,
    upper_ref,
    lower_ref,
    nodes_ref,
    semaphores,
):
    copies = [
        (flow_hbm.at[:, 0:16, :], flow_ref.at[:, 0:16, :]),
        (flow_hbm.at[:, 48:64, :], flow_ref.at[:, 16:32, :]),
        (tangent_hbm.at[:, 0:16, :], tangent_ref.at[:, 0:16, :]),
        (tangent_hbm.at[:, 48:64, :], tangent_ref.at[:, 16:32, :]),
        (places_hbm, places_ref),
        (upper_hbm, upper_ref),
        (lower_hbm, lower_ref),
        (nodes_hbm, nodes_ref),
    ]
    copies = [
        pltpu.make_async_copy(source, target, semaphores.at[i])
        for i, (source, target) in enumerate(copies)
    ]
    for copy in copies:
        copy.start()
    for copy in copies:
        copy.wait()
    odd = on_odd()
    lane = lanes()
    group = lane // 32

    def faces(list_ref, row):
        index = pad_lanes(list_ref[...])
        index = spread(index)
        tiled = index
        for g in range(1, 4):
            tiled = jnp.where(group == g, pltpu.roll(index, 32 * g, 1), tiled)
        chunks = []
        for first in range(0, 12, 4):
            merged = None
            for g in range(4):
                v = first + g
                if v >= 10:
                    continue
                source = flow_ref if v < 5 else tangent_ref
                block = pad_lanes(source[v % 5, row : row + 16, :])
                block = pick(block, tiled)
                own = jnp.concatenate([group, group], axis=0) == g
                merged = jnp.where(own, block, 0.0 if merged is None else merged)
            chunks.append(merged)
        return jnp.concatenate(chunks, axis=0)

    up = faces(upper_ref, 16)
    down = faces(lower_ref, 0)
    node_index = spread(pad_lanes(nodes_ref[...]))
    places = jnp.concatenate([places_ref[...], jnp.zeros((5, 102), F32)], axis=0)
    nodes = pick(pad_lanes(places), node_index)
    none = jnp.zeros((8, 128), F32)
    up = jnp.concatenate([up, none], axis=0)
    down = jnp.concatenate([down, nodes], axis=0)
    a_ref[...] = jnp.where(odd, down, up)
    b_ref[...] = jnp.where(odd, up, down)


def face_pairs(ref, v):
    value = ref[v]
    sides = []
    for s in range(2):
        first = value[48 * s : 48 * s + 16]
        second = jnp.concatenate(
            [value[16 * i + 12 * s : 16 * i + 12 * s + 4] for i in range(4)], axis=0
        )
        third = ref[pl.ds(v, 1), pl.ds(3 * s, 16, stride=4), :][0]
        sides.append(jnp.concatenate([first, second, third], axis=0))
    return pair(sides[0], sides[1])


def volume_pairs(ref, v):
    return pair(ref[v, 0:32, :], ref[v, 32:64, :])


def corner_values(index, own_rows, halo_rows):
    local = index < 102
    own_index = jnp.where(local, index, 0)
    halo_index = jnp.where(local, 0, index - 102)
    result = []
    for i in range(3):
        own = pick(spread(own_rows[i : i + 1]), own_index)
        halo = pick(spread(halo_rows[i : i + 1]), halo_index)
        result.append(jnp.where(local, own, halo))
    return result


def corner_operand(values):
    low = lanes() < 64
    blocks = [
        jnp.concatenate([jnp.where(low, v, 0.0), jnp.where(low, 0.0, v)], axis=0) for v in values
    ]
    return jnp.concatenate(blocks, axis=1)


def columns(array, rows, i):
    return array[rows, 128 * i : 128 * i + 128]


def tangents_of(spans):
    volume = [[columns(spans, slice(32 * j, 32 * j + 32), i) for i in range(3)] for j in range(3)]
    faces = [
        [columns(spans, slice(96 + 48 * w, 144 + 48 * w), i) for i in range(3)] for w in range(2)
    ]
    return volume, faces


def folded(product, v):
    block = product[:, 128 * v : 128 * v + 128]
    return block[0:64] + pltpu.roll(block[64:128], 64, 1)


def side_sign():
    return jnp.where(lanes(48) < 64, -1.0, 1.0).astype(F32)


def ready_kernel(
    flow_ref,
    tangent_ref,
    far_ref,
    places_ref,
    neighbour_ref,
    nodes_ref,
    sends_ref,
    flags_ref,
    damping_ref,
    tables_ref,
    inner_ref,
    state_ref,
    outer_ref,
    places_out,
    border_ref,
    node_index_ref,
    send_index_ref,
    named_ref,
    chosen_ref,
    weight_ref,
    smoothing_ref,
    assemble_ref,
    transposed_ref,
    corner_ref,
    corner_transposed_ref,
):
    lane = lanes()
    low = lane < 64
    neighbours = neighbour_ref[...]
    listed = [
        spread(pair(neighbours[2 * j : 2 * j + 1], neighbours[2 * j + 1 : 2 * j + 2]))
        for j in range(3)
    ]
    border_ref[...] = listed[0]
    local = []
    for j in range(3):
        index = jnp.where(listed[j] < 64, listed[j], 0)
        local.append(jnp.where(low, index + 64, index))
    far = [jnp.concatenate([m, m], axis=0) == 96 for m in listed]
    for v in range(10):
        source = flow_ref if v < 5 else tangent_ref
        inner = face_pairs(source, v % 5)
        inner_ref[v] = inner
        state_ref[v] = volume_pairs(source, v % 5)
        far_value = far_ref[0:1, v : v + 1] if v < 5 else 0.0
        for j in range(3):
            rows = slice(16 * j, 16 * j + 16)
            outer_ref[v, rows, :] = jnp.where(far[j], far_value, pick(inner[rows], local[j]))
    places_out[...] = jnp.concatenate([pad_lanes(places_ref[...]), jnp.zeros((5, 128), F32)], axis=0)
    node_index = pair(nodes_ref[...], nodes_ref[...])
    node_index_ref[...] = node_index
    send_row = pad_lanes(sends_ref[...])
    send_index_ref[...] = spread(send_row)
    table_row = lax.broadcasted_iota(jnp.int32, (256, 128), 0)
    node_of_row = jnp.where(
        table_row < 102, table_row, jnp.where(table_row < 128, -1, table_row - 26)
    )
    for p in range(4):
        named = jnp.where(
            low[0:1], node_index[2 * p : 2 * p + 1], node_index[2 * p + 1 : 2 * p + 2]
        )
        named_ref[:, 128 * p : 128 * p + 128] = (
            (node_of_row == named).astype(F32).astype(jnp.bfloat16)
        )
    sent = jnp.where(lane[0:1] < 51, send_row, -1)
    chosen_ref[...] = (
        (lax.broadcasted_iota(jnp.int32, (128, 128), 0) == sent).astype(F32).astype(jnp.bfloat16)
    )
    weight = flags_ref[...].astype(F32)
    weight_ref[...] = spread(pair(weight, weight))
    smoothing_ref[...] = jnp.where(
        lane == 0, damping_ref[0:1, 0:1], jnp.broadcast_to(damping_ref[0:1, 1:2], (8, 128))
    )
    assemble_ref[...] = tables_ref[0:128, 0:144]
    transposed_ref[...] = tables_ref[128:272, 0:128]
    corner_ref[...] = tables_ref[272:472, 0:16]
    corner_transposed_ref[...] = tables_ref[472:488, 0:192]


class Border:
    def __init__(self, border, lower, upper):
        self.slot = jnp.clip(border - 64, 0, 31)
        halo = (border >= 64) & (border < 96)
        low = lanes() < 64
        self.below = jnp.concatenate([halo & low, halo & low], axis=0)
        self.above = jnp.concatenate([halo & ~low, halo & ~low], axis=0)
        self.lower = lower
        self.upper = upper

    def values(self, local, v):
        rows = slice(16 * (v // 4), 16 * (v // 4) + 16)
        slot = self.slot + 32 * (v % 4)
        first = jnp.where(self.below, pick(self.lower[rows], slot), local[0:16])
        first = jnp.where(self.above, pick(self.upper[rows], slot), first)
        return jnp.concatenate([first, local[16:48]], axis=0)


def geometry(volume_spans, face_spans):
    normals = [cross(volume_spans[(j + 1) % 3], volume_spans[(j + 2) % 3]) for j in range(3)]
    sign = side_sign()
    face_normal = [sign * n for n in cross(face_spans[0], face_spans[1])]
    area_square = sum(n * n for n in face_normal)
    return normals, face_normal, area_square, jnp.sqrt(area_square)


def volume_flux(state, normals):
    prims = primitives(state)
    return [along_flux(prims, normals[j]) for j in range(3)]


def assembled(assemble, fluxes, jump):
    stacked = [
        jnp.concatenate([fluxes[0][v], fluxes[1][v], fluxes[2][v], jump[v]], axis=0)
        for v in range(5)
    ]
    product = dot(assemble, jnp.concatenate(stacked, axis=1))
    return [folded(product, v) for v in range(5)]


def change_kernel(
    inner_ref,
    state_ref,
    local_ref,
    border_ref,
    a_ref,
    b_ref,
    assemble_ref,
    spans_ref,
    outer_ref,
    change_ref,
    token_ref,
):
    odd = on_odd()
    from_a = a_ref[...]
    from_b = b_ref[...]
    border = Border(border_ref[...], jnp.where(odd, from_a, from_b), jnp.where(odd, from_b, from_a))
    volume_spans, face_spans = tangents_of(spans_ref[...])
    normals, face_normal, area_square, area = geometry(volume_spans, face_spans)
    inner = [inner_ref[v] for v in range(5)]
    inner_change = [inner_ref[5 + v] for v in range(5)]
    outer = [outer_ref[v] for v in range(5)]
    outer_change = [border.values(local_ref[5 + v], 5 + v) for v in range(5)]
    _, jump_change = jax.jvp(
        lambda u, w: jump_of(u, w, face_normal, area_square, area),
        (inner, outer),
        (inner_change, outer_change),
    )
    state = [state_ref[v] for v in range(5)]
    state_change = [state_ref[5 + v] for v in range(5)]
    _, flux_changes = jax.jvp(lambda u: volume_flux(u, normals), (state,), (state_change,))
    change = assembled(assemble_ref[...], flux_changes, jump_change)
    for v in range(5):
        change_ref[v] = change[v][:, 0:64]
    token_ref[...] = jnp.zeros((8, 128), F32)


def main_kernel(
    inner_ref,
    state_ref,
    local_ref,
    places_ref,
    border_ref,
    node_index_ref,
    send_index_ref,
    named_ref,
    weight_ref,
    smoothing_ref,
    a_ref,
    b_ref,
    assemble_ref,
    transposed_ref,
    corner_ref,
    corner_transposed_ref,
    residual_ref,
    table_ref,
    send_a_ref,
    send_b_ref,
    spans_ref,
    outer_ref,
    slopes_ref,
):
    odd = on_odd()
    lane = lanes()
    from_a = a_ref[...]
    from_b = b_ref[...]
    lower = jnp.where(odd, from_a, from_b)
    upper = jnp.where(odd, from_b, from_a)

    corners = corner_values(node_index_ref[...], places_ref[...], upper[48:56])
    relative = [c - c[0:1] for c in corners]
    spans = dot(corner_ref[...], corner_operand(relative))
    spans_ref[...] = spans
    volume_spans, face_spans = tangents_of(spans)
    normals, face_normal, area_square, area = geometry(volume_spans, face_spans)
    sign = side_sign()

    inner = [inner_ref[v] for v in range(5)]
    border = Border(border_ref[...], lower, upper)
    outer = [border.values(local_ref[v], v) for v in range(5)]
    for v in range(5):
        outer_ref[v] = outer[v]
    jump = jump_of(inner, outer, face_normal, area_square, area)
    state = [state_ref[v] for v in range(5)]
    residual = assembled(assemble_ref[...], volume_flux(state, normals), jump)
    for v in range(5):
        residual_ref[v] = residual[v][:, 0:64]

    weight = weight_ref[0:1]
    low64 = lanes(64) < 64
    seeds = []
    for v in range(5):
        seed = residual[v] * weight
        seeds.append(
            jnp.concatenate(
                [jnp.where(low64, seed, 0.0), jnp.where(low64, 0.0, pltpu.roll(seed, 64, 1))],
                axis=0,
            )
        )
    back = dot(transposed_ref[...], jnp.concatenate(seeds, axis=1))
    prims = primitives(state)
    normal_bar = []
    for j in range(3):
        cotangent = [columns(back, slice(32 * j, 32 * j + 32), v) for v in range(5)]
        normal_bar.append(along_flux_transposed(prims, cotangent))
    cotangent = [columns(back, slice(96, 144), v) for v in range(5)]
    inner_prims = primitives(inner)
    outer_prims = primitives(outer)
    slopes = wave_gradient(inner_prims, outer_prims, face_normal, area_square, area)
    for i in range(3):
        slopes_ref[i] = slopes[i]
    lift = sum(c * (w - u) for c, w, u in zip(cotangent, outer, inner))
    from_outer = along_flux_transposed(outer_prims, cotangent)
    from_inner = along_flux_transposed(inner_prims, cotangent)
    face_bar = [
        (0.5 * sign) * (from_outer[i] - from_inner[i] - lift * slopes[i]) for i in range(3)
    ]
    span_bar = []
    for j in range(3):
        first = cross(volume_spans[(j + 1) % 3], normal_bar[(j + 2) % 3])
        second = cross(normal_bar[(j + 1) % 3], volume_spans[(j + 2) % 3])
        span_bar.append(added(first, second))
    face_span_bar = [cross(face_spans[1], face_bar), cross(face_bar, face_spans[0])]
    stacked_bar = jnp.concatenate(
        [
            jnp.concatenate(
                [span_bar[j][i] for j in range(3)] + [face_span_bar[w][i] for w in range(2)],
                axis=0,
            )
            for i in range(3)
        ],
        axis=1,
    )
    corner_bar = dot(corner_transposed_ref[...], stacked_bar)
    smoothing = smoothing_ref[0:1, 1:2]
    pieces = []
    for i in range(3):
        block = columns(corner_bar, slice(0, 16), i)
        bar = block[0:8] + pltpu.roll(block[8:16], 64, 1)
        bar = bar + smoothing * weight * columns(spans, slice(192, 200), i)
        pieces.append(bar)
    pieces.append(spread(weight))
    gradient = jnp.concatenate(pieces, axis=0)
    gradient = jnp.where(lanes(32) < 64, gradient, pltpu.roll(gradient, 64, 1))
    row_corner = lax.broadcasted_iota(jnp.int32, (32, 128), 0) % 8
    half = jnp.where(lanes(32) < 64, 0, 1)
    left = [jnp.where(row_corner == 2 * p + half, gradient, 0.0) for p in range(4)]
    scattered = placed(jnp.concatenate(left, axis=1), named_ref[...])
    rows = [jnp.sum(scattered[8 * i : 8 * i + 8], axis=0, keepdims=True) for i in range(4)]
    table = jnp.concatenate(rows + [jnp.zeros((4, 256), F32)], axis=0)
    table_ref[...] = table
    up = table[:, 128:256]
    down = jnp.where(lane < 51, pick(table[:, 0:128], send_index_ref[...]), 0.0)
    send_a_ref[...] = jnp.where(odd, down, up)
    send_b_ref[...] = jnp.where(odd, up, down)


def second_kernel(
    inner_ref,
    state_ref,
    node_index_ref,
    chosen_ref,
    weight_ref,
    smoothing_ref,
    table_ref,
    a_ref,
    b_ref,
    spans_ref,
    outer_ref,
    slopes_ref,
    assemble_ref,
    corner_ref,
    _,
    descent_ref,
    sums_ref,
):
    odd = on_odd()
    lane = lanes()
    from_a = a_ref[...]
    from_b = b_ref[...]
    lower = jnp.where(odd, from_a, from_b)
    upper = jnp.where(odd, from_b, from_a)
    table = table_ref[...]
    sixteen = jnp.concatenate([jnp.where(lane < 51, lower, 0.0), jnp.zeros((8, 128), F32)], axis=0)
    own = table[:, 0:128] + placed(sixteen, chosen_ref[...])[0:8]
    halo = table[:, 128:256] + upper
    own = -jnp.where(own[3:4] > 0.5, own, 0.0)
    halo = -jnp.where(halo[3:4] > 0.5, halo, 0.0)
    descent_ref[...] = own[0:3]
    moved = jnp.where(lax.broadcasted_iota(jnp.int32, (8, 128), 0) < 3, own, 0.0)
    norm = jnp.sum(moved * moved, axis=(0, 1), keepdims=True)

    steps = corner_values(node_index_ref[...], own, halo)
    moves = dot(corner_ref[...], corner_operand(steps))
    volume_moves, face_moves = tangents_of(moves)
    volume_spans, face_spans = tangents_of(spans_ref[...])
    state = primitives([state_ref[v] for v in range(5)])
    fluxes = []
    for j in range(3):
        a, b = (j + 1) % 3, (j + 2) % 3
        normal_move = added(
            cross(volume_moves[a], volume_spans[b]), cross(volume_spans[a], volume_moves[b])
        )
        fluxes.append(along_flux(state, normal_move))
    sign = side_sign()
    face_move = [
        sign * n
        for n in added(cross(face_moves[0], face_spans[1]), cross(face_spans[0], face_moves[1]))
    ]
    inner = [inner_ref[v] for v in range(5)]
    outer = [outer_ref[v] for v in range(5)]
    inner_flux = along_flux(primitives(inner), face_move)
    outer_flux = along_flux(primitives(outer), face_move)
    wave_move = sum(slopes_ref[i] * face_move[i] for i in range(3))
    jump = [
        0.5 * (outer_flux[v] - inner_flux[v] - wave_move * (outer[v] - inner[v]))
        for v in range(5)
    ]
    square = sum(
        change * change for change in assembled(assemble_ref[...], fluxes, jump)
    )
    weight = jnp.where(lane[0:1] < 64, weight_ref[0:1], 0.0)
    curvature = jnp.sum(jnp.sum(square, axis=0, keepdims=True) * weight, axis=1, keepdims=True)
    bend = sum(steps[i] * columns(moves, slice(192, 200), i) for i in range(3))
    bending = smoothing_ref[0:1, 1:2] * jnp.sum(
        jnp.sum(bend, axis=0, keepdims=True) * weight, axis=1, keepdims=True
    )
    lower_sum = curvature + bending + smoothing_ref[0:1, 0:1] * norm
    sums = jnp.where(lane[0:1] == 0, norm, jnp.where(lane[0:1] == 1, lower_sum, 0.0))
    for i in range(sums_ref.shape[0]):
        sums_ref[i] = sums


def finish_kernel(sums_ref, descent_ref, update_ref):
    total = jnp.sum(sums_ref[...], axis=0)
    step = total[:, 0:1] / total[:, 1:2]
    update_ref[...] = step * descent_ref[:, 0:102]


def call(kernel, out_shape, arrays, cost=None, place=pltpu.VMEM, scratch=(), limit=16 << 20):
    vector = pl.BlockSpec(memory_space=pltpu.VMEM)
    return pl.pallas_call(
        kernel,
        out_shape=[
            s if isinstance(s, jax.ShapeDtypeStruct) else jax.ShapeDtypeStruct(s, F32)
            for s in out_shape
        ],
        in_specs=[pl.BlockSpec(memory_space=place)] * len(arrays),
        out_specs=[vector] * len(out_shape),
        scratch_shapes=list(scratch),
        compiler_params=pltpu.CompilerParams(vmem_limit_bytes=limit),
        cost_estimate=cost,
    )(*arrays)


def exchange(value_a, value_b, count):
    b = lax.ppermute(
        value_b,
        "parts",
        [(i, (i - 1) % count if i % 2 == 0 else (i + 1) % count) for i in range(count)],
    )
    a = lax.ppermute(value_a, "parts", [(i, i ^ 1) for i in range(count)])
    return a, b


def step(
    flow_state,
    state_tangent,
    far_field,
    coordinates,
    damping,
    face_neighbour,
    element_nodes,
    upper_sends,
    lower_sends,
    node_sends,
    shock_flags,
):
    count = lax.axis_size("parts")
    sends_row = node_sends.reshape(1, 51)
    flags_row = shock_flags.reshape(1, 64)
    damping_row = damping.reshape(1, 2)
    integer = jnp.int32
    pack_a, pack_b = call(
        pack_kernel,
        [(56, 128)] * 2,
        (
            flow_state,
            state_tangent,
            coordinates,
            upper_sends.reshape(1, 32),
            lower_sends.reshape(1, 32),
            sends_row,
        ),
        place=pltpu.HBM,
        limit=60 * 1024 * 1024,
        scratch=(
            pltpu.VMEM((5, 32, 64), F32),
            pltpu.VMEM((5, 32, 64), F32),
            pltpu.VMEM((3, 102), F32),
            pltpu.VMEM((1, 32), integer),
            pltpu.VMEM((1, 32), integer),
            pltpu.VMEM((1, 51), integer),
            pltpu.SemaphoreType.DMA((8,)),
        ),
    )
    got_a, got_b = exchange(pack_a, pack_b, count)
    (
        inner,
        state,
        local,
        places,
        border,
        node_index,
        send_index,
        named,
        chosen,
        weight,
        smoothing,
        assemble,
        transposed,
        corner,
        corner_transposed,
    ) = call(
        ready_kernel,
        [
            (10, 48, 128),
            (10, 32, 128),
            (10, 48, 128),
            (8, 128),
            jax.ShapeDtypeStruct((8, 128), integer),
            jax.ShapeDtypeStruct((8, 128), integer),
            jax.ShapeDtypeStruct((8, 128), integer),
            jax.ShapeDtypeStruct((256, 512), jnp.bfloat16),
            jax.ShapeDtypeStruct((128, 128), jnp.bfloat16),
            (8, 128),
            (8, 128),
            (128, 144),
            (144, 128),
            (200, 16),
            (16, 192),
        ],
        (
            flow_state,
            state_tangent,
            far_field.reshape(1, 5),
            coordinates,
            face_neighbour,
            element_nodes,
            sends_row,
            flags_row,
            damping_row,
            jnp.asarray(constant_tables()),
        ),
        pl.CostEstimate(flops=200_000_000, bytes_accessed=1_000_000, transcendentals=100_000),
    )
    residual, table, send_a, send_b, spans, outer, slopes = call(
        main_kernel,
        [
            (5, 64, 64),
            (8, 256),
            (8, 128),
            (8, 128),
            (200, 384),
            (5, 48, 128),
            (3, 48, 128),
        ],
        (
            inner,
            state,
            local,
            places,
            border,
            node_index,
            send_index,
            named,
            weight,
            smoothing,
            got_a,
            got_b,
            assemble,
            transposed,
            corner,
            corner_transposed,
        ),
    )
    back_a, back_b = exchange(send_a, send_b, count)
    change, token = call(
        change_kernel,
        [(5, 64, 64), (8, 128)],
        (inner, state, local, border, got_a, got_b, assemble, spans, outer),
        pl.CostEstimate(flops=200_000_000, bytes_accessed=1_000_000, transcendentals=100_000),
    )
    group = min(16, count)
    near = [[base + g for g in range(group)] for base in range(0, count, group)]
    far = [[base + group * g for g in range(count // group)] for base in range(group)]
    descent, sums = call(
        second_kernel,
        [(3, 128), (group, 1, 128)],
        (
            inner,
            state,
            node_index,
            chosen,
            weight,
            smoothing,
            table,
            back_a,
            back_b,
            spans,
            outer,
            slopes,
            assemble,
            corner,
            token,
        ),
    )
    sums = lax.all_to_all(sums, "parts", 0, 0, axis_index_groups=near)
    if count > group:
        sums = jnp.broadcast_to(jnp.sum(sums, axis=0)[None], (count // group, 1, 128))
        sums = lax.all_to_all(sums, "parts", 0, 0, axis_index_groups=far)
    (update,) = call(finish_kernel, [(3, 102)], (sums, descent))
    return (residual, change, update)


def solution(mesh):
    in_specs = (
        P(None, None, "parts"),
        P(None, None, "parts"),
        P(),
        P(None, "parts"),
        P(),
        P(None, "parts"),
        P(None, "parts"),
        P("parts"),
        P("parts"),
        P("parts"),
        P("parts"),
    )
    out_specs = (P(None, None, "parts"), P(None, None, "parts"), P(None, "parts"))
    return jax.shard_map(step, mesh=mesh, in_specs=in_specs, out_specs=out_specs, check_vma=False)
```

```python
import math

import jax
import jax.numpy as jnp
import numpy as np
from jax import lax
from jax.experimental import pallas as pl
from jax.experimental.pallas import tpu as pltpu
from jax.sharding import PartitionSpec as P


GAMMA = 1.4
SOFTENING = 0.01
HIGHEST = lax.Precision.HIGHEST
F32 = jnp.float32


def lobatto_tables():
    points = np.array([-1.0, -math.sqrt(0.2), math.sqrt(0.2), 1.0])
    weights = np.array([1.0, 5.0, 5.0, 1.0]) / 6.0
    derivative = np.zeros((4, 4))
    for a in range(4):
        for b in range(4):
            if a == b:
                derivative[a, b] = sum((1.0 / (points[a] - points[m]) for m in range(4) if m != a))
            else:
                numerator = 1.0
                denominator = 1.0
                for m in range(4):
                    if m != b:
                        denominator *= points[b] - points[m]
                        if m != a:
                            numerator *= points[a] - points[m]
                derivative[a, b] = numerator / denominator
    return (points, weights, derivative)


def shape_gradients():
    points = lobatto_tables()[0]
    gradients = np.zeros((3, 64, 8))
    for q in range(64):
        position = (q // 16, q // 4 % 4, q % 4)
        for k in range(8):
            corner_bits = (k // 4, k // 2 % 2, k % 2)
            for j in range(3):
                factor = 1.0
                for m in range(3):
                    orient = 1.0 if corner_bits[m] == 1 else -1.0
                    if m == j:
                        factor *= 0.5 * orient
                    else:
                        factor *= 0.5 * (1.0 + orient * points[position[m]])
                gradients[j, q, k] = factor
    return gradients


def edge_laplacian():
    matrix = np.zeros((8, 8))
    for k in range(8):
        matrix[k, k] = 3.0
        for b in range(3):
            matrix[k, k ^ 1 << b] = -1.0
    return matrix


def face_rows(j, s):
    rows = [q for q in range(64) if (q // 16, q // 4 % 4, q % 4)[j] == 3 * s]
    return np.array(rows)


def constant_matrices():
    _, weights, derivative = lobatto_tables()
    volume = np.einsum("a,b,c->abc", weights, weights, weights).reshape(64)
    face = np.einsum("a,b->ab", weights, weights).reshape(16)
    eye = np.eye(4)
    full = [
        np.kron(np.kron(derivative, eye), eye),
        np.kron(np.kron(eye, derivative), eye),
        np.kron(np.kron(eye, eye), derivative),
    ]
    assemble = np.zeros((128, 144))
    for half in range(2):
        rows = slice(64 * half, 64 * half + 64)
        for j in range(3):
            weighted = volume[:, None] * full[j]
            assemble[rows, 32 * j : 32 * j + 32] = weighted[:, 32 * half : 32 * half + 32]
            for point, q in enumerate(face_rows(j, half)):
                assemble[64 * half + q, 96 + 16 * j + point] = face[point]
    gradients = shape_gradients()
    corner = np.zeros((200, 16))
    for half in range(2):
        columns = slice(8 * half, 8 * half + 8)
        for j in range(3):
            corner[32 * j : 32 * j + 32, columns] = gradients[j, 32 * half : 32 * half + 32]
            for which in range(2):
                base = 96 + 48 * which + 16 * j
                corner[base : base + 16, columns] = gradients[(j + 1 + which) % 3][
                    face_rows(j, half)
                ]
    corner[192:200, 0:8] = edge_laplacian()
    return assemble.astype(np.float32), corner.astype(np.float32)


def constant_tables():
    assemble, corner = constant_matrices()
    tables = np.zeros((488, 256), np.float32)
    tables[0:128, 0:144] = assemble
    tables[128:272, 0:128] = assemble.T
    tables[272:472, 0:16] = corner
    tables[472:488, 0:192] = corner[0:192].T
    return tables


def dot(a, b):
    return jnp.dot(a, b, precision=HIGHEST, preferred_element_type=F32)


def placed(a, chosen):
    rows = a.shape[0]
    parts = []
    for _ in range(3):
        part = a.astype(jnp.bfloat16)
        parts.append(part)
        a = a - part.astype(F32)
    product = lax.dot_general(
        jnp.concatenate(parts, axis=0),
        chosen,
        (((1,), (1,)), ((), ())),
        preferred_element_type=F32,
    )
    return product[0:rows] + product[rows : 2 * rows] + product[2 * rows : 3 * rows]


def lanes(rows=8):
    return lax.broadcasted_iota(jnp.int32, (rows, 128), 1)


def pair(left, right):
    return jnp.concatenate([left, right], axis=1)


def pick(table, index):
    blocks = [
        jnp.take_along_axis(table[r : r + 8], index, axis=1, mode="promise_in_bounds")
        for r in range(0, table.shape[0], 8)
    ]
    return blocks[0] if len(blocks) == 1 else jnp.concatenate(blocks, axis=0)


def spread(row, rows=8):
    return jnp.broadcast_to(row, (rows, row.shape[1]))


def pad_lanes(value, width=128):
    fill = jnp.zeros((value.shape[0], width - value.shape[1]), value.dtype)
    return jnp.concatenate([value, fill], axis=1)


def primitives(values):
    density = values[0]
    momentum = values[1:4]
    energy = values[4]
    inverse = 1.0 / density
    velocity = [m * inverse for m in momentum]
    kinetic = sum(m * v for m, v in zip(momentum, velocity))
    pressure = (GAMMA - 1.0) * (energy - 0.5 * kinetic)
    return (density, velocity, pressure, momentum, energy + pressure, inverse)


def along_flux(prims, normal):
    density, velocity, pressure, momentum, total, _ = prims
    along = sum(v * n for v, n in zip(velocity, normal))
    return (
        [density * along]
        + [m * along + pressure * n for m, n in zip(momentum, normal)]
        + [total * along]
    )


def along_flux_transposed(prims, cotangent):
    density, velocity, pressure, momentum, total, _ = prims
    scale = density * cotangent[0] + total * cotangent[4]
    for m in range(3):
        scale = scale + momentum[m] * cotangent[1 + m]
    return [velocity[i] * scale + pressure * cotangent[1 + i] for i in range(3)]


def cross(a, b):
    return [
        a[1] * b[2] - a[2] * b[1],
        a[2] * b[0] - a[0] * b[2],
        a[0] * b[1] - a[1] * b[0],
    ]


def added(a, b):
    return [x + y for x, y in zip(a, b)]


def signal_speed(prims, normal, area_square, area):
    _, velocity, pressure, _, _, inverse = prims
    along = sum(v * n for v, n in zip(velocity, normal))
    root = jnp.sqrt(along * along + SOFTENING * area_square)
    sound = jnp.sqrt(GAMMA * pressure * inverse)
    return root + sound * area, along, root, sound


def jump_of(inner, outer, normal, area_square, area):
    inner_prims = primitives(inner)
    outer_prims = primitives(outer)
    inner_speed = signal_speed(inner_prims, normal, area_square, area)[0]
    outer_speed = signal_speed(outer_prims, normal, area_square, area)[0]
    difference = inner_speed - outer_speed
    wave = 0.5 * (inner_speed + outer_speed) + 0.5 * jnp.sqrt(
        difference * difference + SOFTENING * area_square
    )
    inner_flux = along_flux(inner_prims, normal)
    outer_flux = along_flux(outer_prims, normal)
    return [
        0.5 * (outer_flux[v] - inner_flux[v]) - 0.5 * wave * (outer[v] - inner[v])
        for v in range(5)
    ]


def wave_gradient(inner_prims, outer_prims, normal, area_square, area):
    inner_speed, along_u, root_u, sound_u = signal_speed(inner_prims, normal, area_square, area)
    outer_speed, along_w, root_w, sound_w = signal_speed(outer_prims, normal, area_square, area)
    difference = inner_speed - outer_speed
    spread_root = jnp.sqrt(difference * difference + SOFTENING * area_square)
    over_u = 1.0 / root_u
    over_w = 1.0 / root_w
    over_area = 1.0 / area
    over_spread = 0.5 / spread_root
    result = []
    for i in range(3):
        slope_u = (along_u * inner_prims[1][i] + SOFTENING * normal[i]) * over_u + (
            sound_u * over_area
        ) * normal[i]
        slope_w = (along_w * outer_prims[1][i] + SOFTENING * normal[i]) * over_w + (
            sound_w * over_area
        ) * normal[i]
        result.append(
            0.5 * (slope_u + slope_w)
            + (difference * (slope_u - slope_w) + SOFTENING * normal[i]) * over_spread
        )
    return result


def position_bit(bit):
    return ((lax.axis_index("parts") >> bit) & 1) == 1


def pack_kernel(*refs):
    sources = refs[0:10]
    tables_hbm, damping_hbm = refs[10:12]
    (
        a_ref,
        b_ref,
        c_ref,
        d_ref,
        up_ref,
        down_ref,
        flagged_ref,
        sends_out,
        tables_out,
        damping_out,
    ) = refs[12:22]
    held = refs[22:32]
    semaphores = refs[32]
    moves = list(zip(sources, held)) + [(tables_hbm, tables_out), (damping_hbm, damping_out)]
    copies = [
        pltpu.make_async_copy(source, target, semaphores.at[i])
        for i, (source, target) in enumerate(moves)
    ]
    for copy in copies:
        copy.start()
    for copy in copies[0:10]:
        copy.wait()
    (
        flow_ref,
        tangent_ref,
        places_ref,
        upper_ref,
        lower_ref,
        sends_ref,
        neighbour_ref,
        nodes_ref,
        flags_ref,
        far_ref,
    ) = held
    lane = lanes()
    group = lane // 32
    group16 = jnp.concatenate([group, group], axis=0)

    def faces(list_ref, row):
        index = spread(pad_lanes(list_ref[...]))
        tiled = index
        for g in range(1, 4):
            tiled = jnp.where(group == g, pltpu.roll(index, 32 * g, 1), tiled)
        chunks = []
        for first in range(0, 12, 4):
            merged = None
            for g in range(4):
                v = first + g
                if v >= 10:
                    continue
                source = flow_ref if v < 5 else tangent_ref
                block = pick(pad_lanes(source[v % 5, row : row + 16, :]), tiled)
                merged = jnp.where(group16 == g, block, 0.0 if merged is None else merged)
            chunks.append(merged)
        return jnp.concatenate(chunks, axis=0)

    up = faces(upper_ref, 48)
    down = faces(lower_ref, 0)
    sends_row = pad_lanes(sends_ref[...])
    places = pad_lanes(jnp.concatenate([places_ref[...], jnp.zeros((5, 102), F32)], axis=0))
    nodes = pick(places, spread(sends_row))
    row8 = lax.broadcasted_iota(jnp.int32, (8, 128), 0)
    nodes = jnp.where(row8 == 3, spread(sends_row.astype(F32)), nodes)
    none = jnp.zeros((8, 128), F32)
    up = jnp.concatenate([up, none], axis=0)
    down = jnp.concatenate([down, nodes], axis=0)

    flags = pad_lanes(flags_ref[...].astype(F32))
    first_row = lax.broadcasted_iota(jnp.int32, (64, 128), 0)
    rank = jnp.sum(
        jnp.where(lanes(64) <= first_row, jnp.broadcast_to(flags, (64, 128)), 0.0),
        axis=1,
        keepdims=True,
    )
    wanted = (lane % 16).astype(F32)
    before = jnp.sum((rank <= wanted[0:1]).astype(F32), axis=0, keepdims=True)
    weight = (before < 63.5).astype(F32)
    chosen = spread(jnp.minimum(before, 63.0).astype(jnp.int32))
    block = lane // 16

    def merged_blocks(parts):
        result = parts[0]
        for b, part in enumerate(parts[1:]):
            result = jnp.where(block == b + 1, part, result)
        return result

    neighbours = neighbour_ref[...]
    listed = [
        spread(pair(neighbours[2 * j : 2 * j + 1], neighbours[2 * j + 1 : 2 * j + 2]))
        for j in range(3)
    ]
    beside = []
    for j in range(3):
        sides = []
        for side in range(2):
            code = pick(listed[j], chosen + 64 * side)
            local = jnp.where(code < 64, code, 0) + (64 if side == 0 else 0)
            sides.append((code == 96, local))
        beside.append(sides)
    packed = []
    for v in range(5):
        value = pad_lanes(flow_ref[v])
        packed.append(
            merged_blocks([pick(value[8 * b : 8 * b + 8], chosen) for b in range(8)])
        )
    for v in range(5):
        inner = face_pairs(flow_ref, v)
        far_value = far_ref[0:1, v : v + 1]
        for first in (0, 4):
            parts = []
            for b in range(8):
                chunk, side = first + b % 4, b // 4
                if chunk >= 6:
                    parts.append(none)
                    continue
                far, local = beside[chunk // 2][side]
                taken = pick(inner[8 * chunk : 8 * chunk + 8], local)
                parts.append(jnp.where(far, far_value, taken))
            packed.append(merged_blocks(parts))
    node_index = pick(pair(nodes_ref[...], nodes_ref[...]), chosen)
    local_node = jnp.where(node_index < 102, node_index, 0)
    codes = jnp.where(
        row8 == 0,
        pick(listed[0], chosen).astype(F32),
        jnp.where(row8 == 1, pick(listed[0], chosen + 64).astype(F32), spread(weight)),
    )
    packed.append(
        merged_blocks(
            [pick(spread(places[i : i + 1]), local_node) for i in range(3)]
            + [node_index.astype(F32), codes]
        )
    )
    flagged = jnp.concatenate(packed, axis=0)
    flagged_ref[...] = flagged
    sends_out[...] = sends_ref[...]
    up_ref[...] = up
    down_ref[...] = down
    odd = position_bit(0)
    second = position_bit(1)
    a_ref[0:56] = jnp.where(odd, down, up)
    b_ref[0:56] = jnp.where(odd, up, down)
    a_ref[56:184] = flagged
    b_ref[56:184] = flagged
    short_up = jnp.concatenate([up[0:32], up[48:56]], axis=0)
    short_down = jnp.concatenate([down[0:32], down[48:56]], axis=0)
    c_ref[...] = jnp.where(second, short_down, short_up)
    d_ref[...] = jnp.where(second, short_up, short_down)
    for copy in copies[10:12]:
        copy.wait()


def face_pairs(ref, v):
    value = ref[v]
    sides = []
    for s in range(2):
        first = value[48 * s : 48 * s + 16]
        second = jnp.concatenate(
            [value[16 * i + 12 * s : 16 * i + 12 * s + 4] for i in range(4)], axis=0
        )
        third = ref[pl.ds(v, 1), pl.ds(3 * s, 16, stride=4), :][0]
        sides.append(jnp.concatenate([first, second, third], axis=0))
    return pair(sides[0], sides[1])


def volume_pairs(ref, v):
    return pair(ref[v, 0:32, :], ref[v, 32:64, :])


def corner_values(index, own_rows, halo_rows):
    local = index < 102
    own_index = jnp.where(local, index, 0)
    halo_index = jnp.where(local, 0, index - 102)
    result = []
    for i in range(3):
        own = pick(spread(own_rows[i : i + 1]), own_index)
        halo = pick(spread(halo_rows[i : i + 1]), halo_index)
        result.append(jnp.where(local, own, halo))
    return result


def corner_operand(values):
    low = lanes() < 64
    blocks = [
        jnp.concatenate([jnp.where(low, v, 0.0), jnp.where(low, 0.0, v)], axis=0) for v in values
    ]
    return jnp.concatenate(blocks, axis=1)


def columns(array, rows, i):
    return array[rows, 128 * i : 128 * i + 128]


def tangents_of(spans):
    volume = [[columns(spans, slice(32 * j, 32 * j + 32), i) for i in range(3)] for j in range(3)]
    faces = [
        [columns(spans, slice(96 + 48 * w, 144 + 48 * w), i) for i in range(3)] for w in range(2)
    ]
    return volume, faces


def folded(product, v):
    block = product[:, 128 * v : 128 * v + 128]
    return block[0:64] + pltpu.roll(block[64:128], 64, 1)


def side_sign():
    return jnp.where(lanes(48) < 64, -1.0, 1.0).astype(F32)


def ready_kernel(
    flow_ref,
    tangent_ref,
    far_ref,
    places_ref,
    neighbour_ref,
    nodes_ref,
    tables_ref,
    inner_ref,
    state_ref,
    outer_ref,
    places_out,
    border_ref,
    node_index_ref,
    assemble_ref,
    corner_ref,
):
    lane = lanes()
    low = lane < 64
    neighbours = neighbour_ref[...]
    listed = [
        spread(pair(neighbours[2 * j : 2 * j + 1], neighbours[2 * j + 1 : 2 * j + 2]))
        for j in range(3)
    ]
    border_ref[...] = listed[0]
    local = []
    for j in range(3):
        index = jnp.where(listed[j] < 64, listed[j], 0)
        local.append(jnp.where(low, index + 64, index))
    far = [jnp.concatenate([m, m], axis=0) == 96 for m in listed]
    for v in range(10):
        source = flow_ref if v < 5 else tangent_ref
        inner = face_pairs(source, v % 5)
        inner_ref[v] = inner
        state_ref[v] = volume_pairs(source, v % 5)
        far_value = far_ref[0:1, v : v + 1] if v < 5 else 0.0
        for j in range(3):
            rows = slice(16 * j, 16 * j + 16)
            outer_ref[v, rows, :] = jnp.where(far[j], far_value, pick(inner[rows], local[j]))
    places_out[...] = jnp.concatenate([pad_lanes(places_ref[...]), jnp.zeros((5, 128), F32)], axis=0)
    node_index = pair(nodes_ref[...], nodes_ref[...])
    node_index_ref[...] = node_index
    assemble_ref[...] = tables_ref[0:128, 0:144]
    corner_ref[...] = tables_ref[272:472, 0:16]


class Border:
    def __init__(self, border, lower, upper):
        self.slot = jnp.clip(border - 64, 0, 31)
        halo = (border >= 64) & (border < 96)
        low = lanes() < 64
        self.below = jnp.concatenate([halo & low, halo & low], axis=0)
        self.above = jnp.concatenate([halo & ~low, halo & ~low], axis=0)
        self.lower = lower
        self.upper = upper

    def values(self, local, v):
        rows = slice(16 * (v // 4), 16 * (v // 4) + 16)
        slot = self.slot + 32 * (v % 4)
        first = jnp.where(self.below, pick(self.lower[rows], slot), local[0:16])
        first = jnp.where(self.above, pick(self.upper[rows], slot), first)
        return jnp.concatenate([first, local[16:48]], axis=0)


def geometry(volume_spans, face_spans):
    normals = [cross(volume_spans[(j + 1) % 3], volume_spans[(j + 2) % 3]) for j in range(3)]
    sign = side_sign()
    face_normal = [sign * n for n in cross(face_spans[0], face_spans[1])]
    area_square = sum(n * n for n in face_normal)
    return normals, face_normal, area_square, jnp.sqrt(area_square)


def volume_flux(state, normals):
    prims = primitives(state)
    return [along_flux(prims, normals[j]) for j in range(3)]


def assembled(assemble, fluxes, jump):
    stacked = [
        jnp.concatenate([fluxes[0][v], fluxes[1][v], fluxes[2][v], jump[v]], axis=0)
        for v in range(5)
    ]
    product = dot(assemble, jnp.concatenate(stacked, axis=1))
    return [folded(product, v) for v in range(5)]


def plane_kernel(
    inner_ref,
    state_ref,
    local_ref,
    places_ref,
    border_ref,
    node_index_ref,
    a_ref,
    b_ref,
    assemble_ref,
    corner_ref,
    residual_ref,
    change_ref,
):
    odd = position_bit(0)
    from_a = a_ref[0:56]
    from_b = b_ref[0:56]
    lower = jnp.where(odd, from_a, from_b)
    upper = jnp.where(odd, from_b, from_a)
    border = Border(border_ref[...], lower, upper)
    corners = corner_values(node_index_ref[...], places_ref[...], upper[48:56])
    spans = dot(corner_ref[...], corner_operand([c - c[0:1] for c in corners]))
    volume_spans, face_spans = tangents_of(spans)
    normals, face_normal, area_square, area = geometry(volume_spans, face_spans)
    inner = [inner_ref[v] for v in range(10)]
    outer = [border.values(local_ref[v], v) for v in range(10)]
    jump, jump_change = jax.jvp(
        lambda u, w: jump_of(u, w, face_normal, area_square, area),
        (inner[:5], outer[:5]),
        (inner[5:], outer[5:]),
    )
    state = [state_ref[v] for v in range(10)]
    fluxes, flux_changes = jax.jvp(
        lambda u: volume_flux(u, normals), (state[:5],), (state[5:],)
    )
    residual = assembled(assemble_ref[...], fluxes, jump)
    change = assembled(assemble_ref[...], flux_changes, jump_change)
    for v in range(5):
        residual_ref[v] = residual[v][:, 0:64]
        change_ref[v] = change[v][:, 0:64]


def core_kernel(
    a_ref,
    b_ref,
    c_ref,
    d_ref,
    up_ref,
    down_ref,
    flagged_ref,
    sends_ref,
    tables_ref,
    damping_ref,
    descent_ref,
    sums_ref,
    whole_ref,
):
    odd = position_bit(0)
    second = position_bit(1)
    lower = jnp.where(odd, a_ref[...], b_ref[...])
    upper = jnp.where(odd, b_ref[...], a_ref[...])
    lower_two = jnp.where(second, c_ref[...], d_ref[...])
    upper_two = jnp.where(second, d_ref[...], c_ref[...])
    up = up_ref[...]
    down = down_ref[...]
    flagged = flagged_ref[...]
    lane = lanes()
    low = lane < 64
    seat = lane % 16
    block = (lane % 64) // 16

    def three(own, below, above):
        return jnp.where(block == 1, below, jnp.where(block == 2, above, own))

    def taken(row, index):
        rows = slice(row, row + 8)
        moved = slice(56 + row, 64 + row)
        return three(
            pick(flagged[rows], index), pick(lower[moved], index), pick(upper[moved], index)
        )

    for v in range(5):
        for r in range(8):
            whole_ref[v, 8 * r : 8 * r + 8, :] = taken(8 * v, seat + 16 * r)
    state = []
    inner = []
    for v in range(5):
        value = whole_ref[v]
        state.append(jnp.where(lanes(32) < 64, value[0:32], value[32:64]))
        sides = []
        for s in range(2):
            middle = jnp.concatenate(
                [value[16 * i + 12 * s : 16 * i + 12 * s + 4] for i in range(4)], axis=0
            )
            last = whole_ref[pl.ds(v, 1), pl.ds(3 * s, 16, stride=4), :][0]
            sides.append(jnp.concatenate([value[48 * s : 48 * s + 16], middle, last], axis=0))
        inner.append(jnp.where(lanes(48) < 64, sides[0], sides[1]))
    codes = taken(120, seat + 64)
    border = spread(jnp.where(low[0:1], codes[0:1], codes[1:2])).astype(jnp.int32)
    weight = jnp.where(block[0:1] == 3, 0.0, codes[2:3])
    slot = jnp.clip(border - 64, 0, 31)
    halo = (border >= 64) & (border < 96)
    outer = []
    for v in range(5):
        chunks = []
        for chunk in range(6):
            index = seat + 16 * (chunk % 4) + jnp.where(low, 0, 64)
            value = taken(40 + 16 * v + 8 * (chunk // 4), index)
            if chunk < 2:
                rows = slice(16 * (v // 4) + 8 * chunk, 16 * (v // 4) + 8 * chunk + 8)
                at = slot + 32 * (v % 4)
                side0 = three(pick(lower[rows], at), pick(lower_two[rows], at), pick(up[rows], at))
                side1 = three(
                    pick(upper[rows], at), pick(down[rows], at), pick(upper_two[rows], at)
                )
                value = jnp.where(halo, jnp.where(low, side0, side1), value)
            chunks.append(value)
        outer.append(jnp.concatenate(chunks, axis=0))
    node_index = taken(120, seat + 48).astype(jnp.int32)
    foreign = node_index >= 102
    foreign_slot = jnp.where(foreign, node_index - 102, 0)
    corners = []
    for i in range(3):
        local = taken(120, seat + 16 * i)
        remote = three(
            pick(spread(upper[48 + i : 49 + i]), foreign_slot),
            pick(spread(down[48 + i : 49 + i]), foreign_slot),
            pick(spread(upper_two[32 + i : 33 + i]), foreign_slot),
        )
        corners.append(jnp.where(foreign, remote, local))

    spans = dot(tables_ref[272:472, 0:16], corner_operand([c - c[0:1] for c in corners]))
    volume_spans, face_spans = tangents_of(spans)
    normals, face_normal, area_square, area = geometry(volume_spans, face_spans)
    sign = side_sign()
    jump = jump_of(inner, outer, face_normal, area_square, area)
    residual = assembled(tables_ref[0:128, 0:144], volume_flux(state, normals), jump)
    low64 = lanes(64) < 64
    seeds = []
    for v in range(5):
        seed = residual[v] * weight
        seeds.append(
            jnp.concatenate(
                [jnp.where(low64, seed, 0.0), jnp.where(low64, 0.0, pltpu.roll(seed, 64, 1))],
                axis=0,
            )
        )
    back = dot(tables_ref[128:272, 0:128], jnp.concatenate(seeds, axis=1))
    prims = primitives(state)
    normal_bar = []
    for j in range(3):
        cotangent = [columns(back, slice(32 * j, 32 * j + 32), v) for v in range(5)]
        normal_bar.append(along_flux_transposed(prims, cotangent))
    cotangent = [columns(back, slice(96, 144), v) for v in range(5)]
    inner_prims = primitives(inner)
    outer_prims = primitives(outer)
    slopes = wave_gradient(inner_prims, outer_prims, face_normal, area_square, area)
    lift = sum(c * (w - u) for c, w, u in zip(cotangent, outer, inner))
    from_outer = along_flux_transposed(outer_prims, cotangent)
    from_inner = along_flux_transposed(inner_prims, cotangent)
    face_bar = [
        (0.5 * sign) * (from_outer[i] - from_inner[i] - lift * slopes[i]) for i in range(3)
    ]
    span_bar = []
    for j in range(3):
        first = cross(volume_spans[(j + 1) % 3], normal_bar[(j + 2) % 3])
        second = cross(normal_bar[(j + 1) % 3], volume_spans[(j + 2) % 3])
        span_bar.append(added(first, second))
    face_span_bar = [cross(face_spans[1], face_bar), cross(face_bar, face_spans[0])]
    stacked_bar = jnp.concatenate(
        [
            jnp.concatenate(
                [span_bar[j][i] for j in range(3)] + [face_span_bar[w][i] for w in range(2)],
                axis=0,
            )
            for i in range(3)
        ],
        axis=1,
    )
    corner_bar = dot(tables_ref[472:488, 0:192], stacked_bar)
    smoothing = damping_ref[0:1, 1:2]
    pieces = []
    for i in range(3):
        halves = columns(corner_bar, slice(0, 16), i)
        bar = halves[0:8] + pltpu.roll(halves[8:16], 64, 1)
        bar = bar + smoothing * weight * columns(spans, slice(192, 200), i)
        pieces.append(bar)
    pieces.append(spread(weight))
    gradient = jnp.concatenate(pieces, axis=0)
    gradient = jnp.where(lanes(32) < 64, gradient, pltpu.roll(gradient, 64, 1))
    row_corner = lax.broadcasted_iota(jnp.int32, (32, 128), 0) % 8
    half = jnp.where(lanes(32) < 64, 0, 1)
    sent_here = pick(spread(pad_lanes(sends_ref[...])), foreign_slot)
    nowhere = jnp.full((8, 128), -1, jnp.int32)
    own_node = three(
        jnp.where(foreign, -1, node_index), jnp.where(foreign, sent_here, -1), nowhere
    )
    own_node = jnp.where(block == 3, -1, own_node)
    halo_node = jnp.where(block == 0, jnp.where(foreign, node_index - 102, -1), nowhere)
    upper_node = jnp.where((block == 2) & ~foreign, node_index, -1)
    square_row = lax.broadcasted_iota(jnp.int32, (128, 128), 0)
    upper_sends = jnp.where(lane[0:1] < 51, upper[51:52], -5.0)
    upper_column = jnp.sum(
        jnp.where(square_row == lanes(128), jnp.broadcast_to(upper_sends, (128, 128)), 0.0),
        axis=1,
        keepdims=True,
    ).astype(jnp.int32)
    left = []
    right = []
    for p in range(4):
        left.append(jnp.where(row_corner == 2 * p + half, gradient, 0.0))

        def row_of(index):
            return jnp.where(low[0:1], index[2 * p : 2 * p + 1], index[2 * p + 1 : 2 * p + 2])

        own_hit = square_row == row_of(own_node)
        halo_hit = (square_row == row_of(halo_node)) | (upper_column == row_of(upper_node))
        right.append(
            jnp.concatenate([own_hit.astype(F32), halo_hit.astype(F32)], axis=0).astype(
                jnp.bfloat16
            )
        )
    scattered = placed(jnp.concatenate(left, axis=1), jnp.concatenate(right, axis=1))
    rows = [jnp.sum(scattered[8 * i : 8 * i + 8], axis=0, keepdims=True) for i in range(4)]
    table = jnp.concatenate(rows + [jnp.zeros((4, 256), F32)], axis=0)
    own = table[:, 0:128]
    halo_table = table[:, 128:256]
    own = -jnp.where(own[3:4] > 0.5, own, 0.0)
    halo_table = -jnp.where(halo_table[3:4] > 0.5, halo_table, 0.0)
    descent_ref[...] = own[0:3]
    moved = jnp.where(lax.broadcasted_iota(jnp.int32, (8, 128), 0) < 3, own, 0.0)
    norm = jnp.sum(moved * moved, axis=(0, 1), keepdims=True)

    steps = corner_values(node_index, own, halo_table)
    moves = dot(tables_ref[272:472, 0:16], corner_operand(steps))
    volume_moves, face_moves = tangents_of(moves)
    fluxes = []
    for j in range(3):
        a, b = (j + 1) % 3, (j + 2) % 3
        normal_move = added(
            cross(volume_moves[a], volume_spans[b]), cross(volume_spans[a], volume_moves[b])
        )
        fluxes.append(along_flux(prims, normal_move))
    face_move = [
        sign * n
        for n in added(cross(face_moves[0], face_spans[1]), cross(face_spans[0], face_moves[1]))
    ]
    inner_flux = along_flux(inner_prims, face_move)
    outer_flux = along_flux(outer_prims, face_move)
    wave_move = sum(slopes[i] * face_move[i] for i in range(3))
    jump = [
        0.5 * (outer_flux[v] - inner_flux[v] - wave_move * (outer[v] - inner[v]))
        for v in range(5)
    ]
    square = sum(change * change for change in assembled(tables_ref[0:128, 0:144], fluxes, jump))
    own_weight = jnp.where(lane[0:1] < 16, weight, 0.0)
    curvature = jnp.sum(
        jnp.sum(square, axis=0, keepdims=True) * own_weight, axis=1, keepdims=True
    )
    bend = sum(steps[i] * columns(moves, slice(192, 200), i) for i in range(3))
    bending = smoothing * jnp.sum(
        jnp.sum(bend, axis=0, keepdims=True) * own_weight, axis=1, keepdims=True
    )
    lower_sum = curvature + bending + damping_ref[0:1, 0:1] * norm
    sums = jnp.where(lane[0:1] == 0, norm, jnp.where(lane[0:1] == 1, lower_sum, 0.0))
    for i in range(sums_ref.shape[0]):
        sums_ref[i] = sums


def finish_kernel(sums_ref, descent_ref, update_ref):
    total = jnp.sum(sums_ref[...], axis=0)
    step = total[:, 0:1] / total[:, 1:2]
    update_ref[...] = step * descent_ref[:, 0:102]


def call(kernel, out_shape, arrays, cost=None, places=None, scratch=(), limit=16 << 20):
    vector = pl.BlockSpec(memory_space=pltpu.VMEM)
    return pl.pallas_call(
        kernel,
        out_shape=[
            s if isinstance(s, jax.ShapeDtypeStruct) else jax.ShapeDtypeStruct(s, F32)
            for s in out_shape
        ],
        in_specs=[pl.BlockSpec(memory_space=p) for p in places or [pltpu.VMEM] * len(arrays)],
        out_specs=[vector] * len(out_shape),
        scratch_shapes=list(scratch),
        compiler_params=pltpu.CompilerParams(vmem_limit_bytes=limit),
        cost_estimate=cost,
    )(*arrays)


def beyond(i, count):
    return (i - 1) % count if i % 2 == 0 else (i + 1) % count


def beyond_two(i, count):
    return (i - 2) % count if i // 2 % 2 == 0 else (i + 2) % count


def swapped(value, partner):
    count = lax.axis_size("parts")
    return lax.ppermute(value, "parts", [(i, partner(i)) for i in range(count)])


def stays(value):
    return pltpu.with_memory_space_constraint(value, pltpu.HBM)


def step(
    flow_state,
    state_tangent,
    far_field,
    coordinates,
    damping,
    face_neighbour,
    element_nodes,
    upper_sends,
    lower_sends,
    node_sends,
    shock_flags,
):
    count = lax.axis_size("parts")
    sends_row = node_sends.reshape(1, 51)
    flags_row = shock_flags.reshape(1, 64)
    damping_row = damping.reshape(1, 2)
    integer = jnp.int32
    tables = jnp.asarray(constant_tables())
    pack_a, pack_b, pack_c, pack_d, up, down, flagged, sends, held_tables, held_damping = call(
        pack_kernel,
        [(184, 128)] * 2 + [(40, 128)] * 2 + [(56, 128)] * 2
        + [(128, 128), jax.ShapeDtypeStruct((1, 51), integer), (488, 256), (1, 2)],
        tuple(
            stays(x)
            for x in (
                flow_state,
                state_tangent,
                coordinates,
                upper_sends.reshape(1, 32),
                lower_sends.reshape(1, 32),
                sends_row,
                face_neighbour,
                element_nodes,
                flags_row,
                far_field.reshape(1, 5),
                tables,
                damping_row,
            )
        ),
        places=[pltpu.HBM] * 12,
        scratch=(
            pltpu.VMEM((5, 64, 64), F32),
            pltpu.VMEM((5, 64, 64), F32),
            pltpu.VMEM((3, 102), F32),
            pltpu.VMEM((1, 32), integer),
            pltpu.VMEM((1, 32), integer),
            pltpu.VMEM((1, 51), integer),
            pltpu.VMEM((6, 64), integer),
            pltpu.VMEM((8, 64), integer),
            pltpu.VMEM((1, 64), integer),
            pltpu.VMEM((1, 5), F32),
            pltpu.SemaphoreType.DMA((12,)),
        ),
    )
    got_d = swapped(pack_d, lambda i: beyond_two(i, count))
    got_b = swapped(pack_b, lambda i: beyond(i, count))
    got_c = swapped(pack_c, lambda i: i ^ 2)
    got_a = swapped(pack_a, lambda i: i ^ 1)
    (
        inner,
        state,
        local,
        places,
        border,
        node_index,
        assemble,
        corner,
    ) = call(
        ready_kernel,
        [
            (10, 48, 128),
            (10, 32, 128),
            (10, 48, 128),
            (8, 128),
            jax.ShapeDtypeStruct((8, 128), integer),
            jax.ShapeDtypeStruct((8, 128), integer),
            (128, 144),
            (200, 16),
        ],
        (
            flow_state,
            state_tangent,
            far_field.reshape(1, 5),
            coordinates,
            face_neighbour,
            element_nodes,
            held_tables,
        ),
        pl.CostEstimate(flops=200_000_000, bytes_accessed=1_000_000, transcendentals=100_000),
    )
    group = min(16, count)
    near = [[base + g for g in range(group)] for base in range(0, count, group)]
    far = [[base + group * g for g in range(count // group)] for base in range(group)]
    descent, sums = call(
        core_kernel,
        [(3, 128), (group, 1, 128)],
        (
            got_a,
            got_b,
            got_c,
            got_d,
            up,
            down,
            flagged,
            sends,
            held_tables,
            held_damping,
        ),
        scratch=(pltpu.VMEM((5, 64, 128), F32),),
    )
    residual, change = call(
        plane_kernel,
        [(5, 64, 64)] * 2,
        (
            inner,
            state,
            local,
            places,
            border,
            node_index,
            got_a,
            got_b,
            assemble,
            corner,
        ),
        pl.CostEstimate(flops=200_000_000, bytes_accessed=1_000_000, transcendentals=100_000),
    )
    sums = lax.all_to_all(sums, "parts", 0, 0, axis_index_groups=near)
    if count > group:
        sums = jnp.broadcast_to(jnp.sum(sums, axis=0)[None], (count // group, 1, 128))
        sums = lax.all_to_all(sums, "parts", 0, 0, axis_index_groups=far)
    (update,) = call(finish_kernel, [(3, 102)], (sums, descent))
    return (residual, change, update)


def solution(mesh):
    in_specs = (
        P(None, None, "parts"),
        P(None, None, "parts"),
        P(),
        P(None, "parts"),
        P(),
        P(None, "parts"),
        P(None, "parts"),
        P("parts"),
        P("parts"),
        P("parts"),
        P("parts"),
    )
    out_specs = (P(None, None, "parts"), P(None, None, "parts"), P(None, "parts"))
    return jax.shard_map(step, mesh=mesh, in_specs=in_specs, out_specs=out_specs, check_vma=False)
```

```python
import math

import jax
import jax.numpy as jnp
import numpy as np
from jax import lax
from jax.experimental import pallas as pl
from jax.experimental.pallas import tpu as pltpu
from jax.sharding import PartitionSpec as P


GAMMA = 1.4
SOFTENING = 0.01
HIGHEST = lax.Precision.HIGHEST
F32 = jnp.float32


def lobatto_tables():
    points = np.array([-1.0, -math.sqrt(0.2), math.sqrt(0.2), 1.0])
    weights = np.array([1.0, 5.0, 5.0, 1.0]) / 6.0
    derivative = np.zeros((4, 4))
    for a in range(4):
        for b in range(4):
            if a == b:
                derivative[a, b] = sum((1.0 / (points[a] - points[m]) for m in range(4) if m != a))
            else:
                numerator = 1.0
                denominator = 1.0
                for m in range(4):
                    if m != b:
                        denominator *= points[b] - points[m]
                        if m != a:
                            numerator *= points[a] - points[m]
                derivative[a, b] = numerator / denominator
    return (points, weights, derivative)


def shape_gradients():
    points = lobatto_tables()[0]
    gradients = np.zeros((3, 64, 8))
    for q in range(64):
        position = (q // 16, q // 4 % 4, q % 4)
        for k in range(8):
            corner_bits = (k // 4, k // 2 % 2, k % 2)
            for j in range(3):
                factor = 1.0
                for m in range(3):
                    orient = 1.0 if corner_bits[m] == 1 else -1.0
                    if m == j:
                        factor *= 0.5 * orient
                    else:
                        factor *= 0.5 * (1.0 + orient * points[position[m]])
                gradients[j, q, k] = factor
    return gradients


def edge_laplacian():
    matrix = np.zeros((8, 8))
    for k in range(8):
        matrix[k, k] = 3.0
        for b in range(3):
            matrix[k, k ^ 1 << b] = -1.0
    return matrix


def face_rows(j, s):
    rows = [q for q in range(64) if (q // 16, q // 4 % 4, q % 4)[j] == 3 * s]
    return np.array(rows)


def constant_matrices():
    _, weights, derivative = lobatto_tables()
    volume = np.einsum("a,b,c->abc", weights, weights, weights).reshape(64)
    face = np.einsum("a,b->ab", weights, weights).reshape(16)
    eye = np.eye(4)
    full = [
        np.kron(np.kron(derivative, eye), eye),
        np.kron(np.kron(eye, derivative), eye),
        np.kron(np.kron(eye, eye), derivative),
    ]
    assemble = np.zeros((128, 144))
    for half in range(2):
        rows = slice(64 * half, 64 * half + 64)
        for j in range(3):
            weighted = volume[:, None] * full[j]
            assemble[rows, 32 * j : 32 * j + 32] = weighted[:, 32 * half : 32 * half + 32]
            for point, q in enumerate(face_rows(j, half)):
                assemble[64 * half + q, 96 + 16 * j + point] = face[point]
    gradients = shape_gradients()
    corner = np.zeros((200, 16))
    for half in range(2):
        columns = slice(8 * half, 8 * half + 8)
        for j in range(3):
            corner[32 * j : 32 * j + 32, columns] = gradients[j, 32 * half : 32 * half + 32]
            for which in range(2):
                base = 96 + 48 * which + 16 * j
                corner[base : base + 16, columns] = gradients[(j + 1 + which) % 3][
                    face_rows(j, half)
                ]
    corner[192:200, 0:8] = edge_laplacian()
    return assemble.astype(np.float32), corner.astype(np.float32)


def constant_tables():
    assemble, corner = constant_matrices()
    tables = np.zeros((488, 256), np.float32)
    tables[0:128, 0:144] = assemble
    tables[128:272, 0:128] = assemble.T
    tables[272:472, 0:16] = corner
    tables[472:488, 0:192] = corner[0:192].T
    return tables


def dot(a, b):
    return jnp.dot(a, b, precision=HIGHEST, preferred_element_type=F32)


def placed(a, chosen):
    rows = a.shape[0]
    parts = []
    for _ in range(3):
        part = a.astype(jnp.bfloat16)
        parts.append(part)
        a = a - part.astype(F32)
    product = lax.dot_general(
        jnp.concatenate(parts, axis=0),
        chosen,
        (((1,), (1,)), ((), ())),
        preferred_element_type=F32,
    )
    return product[0:rows] + product[rows : 2 * rows] + product[2 * rows : 3 * rows]


def lanes(rows=8):
    return lax.broadcasted_iota(jnp.int32, (rows, 128), 1)


def pair(left, right):
    return jnp.concatenate([left, right], axis=1)


def pick(table, index):
    blocks = [
        jnp.take_along_axis(table[r : r + 8], index, axis=1, mode="promise_in_bounds")
        for r in range(0, table.shape[0], 8)
    ]
    return blocks[0] if len(blocks) == 1 else jnp.concatenate(blocks, axis=0)


def spread(row, rows=8):
    return jnp.broadcast_to(row, (rows, row.shape[1]))


def pad_lanes(value, width=128):
    fill = jnp.zeros((value.shape[0], width - value.shape[1]), value.dtype)
    return jnp.concatenate([value, fill], axis=1)


def primitives(values):
    density = values[0]
    momentum = values[1:4]
    energy = values[4]
    inverse = 1.0 / density
    velocity = [m * inverse for m in momentum]
    kinetic = sum(m * v for m, v in zip(momentum, velocity))
    pressure = (GAMMA - 1.0) * (energy - 0.5 * kinetic)
    return (density, velocity, pressure, momentum, energy + pressure, inverse)


def along_flux(prims, normal):
    density, velocity, pressure, momentum, total, _ = prims
    along = sum(v * n for v, n in zip(velocity, normal))
    return (
        [density * along]
        + [m * along + pressure * n for m, n in zip(momentum, normal)]
        + [total * along]
    )


def along_flux_transposed(prims, cotangent):
    density, velocity, pressure, momentum, total, _ = prims
    scale = density * cotangent[0] + total * cotangent[4]
    for m in range(3):
        scale = scale + momentum[m] * cotangent[1 + m]
    return [velocity[i] * scale + pressure * cotangent[1 + i] for i in range(3)]


def cross(a, b):
    return [
        a[1] * b[2] - a[2] * b[1],
        a[2] * b[0] - a[0] * b[2],
        a[0] * b[1] - a[1] * b[0],
    ]


def added(a, b):
    return [x + y for x, y in zip(a, b)]


def signal_speed(prims, normal, area_square, area):
    _, velocity, pressure, _, _, inverse = prims
    along = sum(v * n for v, n in zip(velocity, normal))
    root = jnp.sqrt(along * along + SOFTENING * area_square)
    sound = jnp.sqrt(GAMMA * pressure * inverse)
    return root + sound * area, along, root, sound


def jump_of(inner, outer, normal, area_square, area):
    inner_prims = primitives(inner)
    outer_prims = primitives(outer)
    inner_speed = signal_speed(inner_prims, normal, area_square, area)[0]
    outer_speed = signal_speed(outer_prims, normal, area_square, area)[0]
    difference = inner_speed - outer_speed
    wave = 0.5 * (inner_speed + outer_speed) + 0.5 * jnp.sqrt(
        difference * difference + SOFTENING * area_square
    )
    inner_flux = along_flux(inner_prims, normal)
    outer_flux = along_flux(outer_prims, normal)
    return [
        0.5 * (outer_flux[v] - inner_flux[v]) - 0.5 * wave * (outer[v] - inner[v])
        for v in range(5)
    ]


def wave_gradient(inner_prims, outer_prims, normal, area_square, area):
    inner_speed, along_u, root_u, sound_u = signal_speed(inner_prims, normal, area_square, area)
    outer_speed, along_w, root_w, sound_w = signal_speed(outer_prims, normal, area_square, area)
    difference = inner_speed - outer_speed
    spread_root = jnp.sqrt(difference * difference + SOFTENING * area_square)
    over_u = 1.0 / root_u
    over_w = 1.0 / root_w
    over_area = 1.0 / area
    over_spread = 0.5 / spread_root
    result = []
    for i in range(3):
        slope_u = (along_u * inner_prims[1][i] + SOFTENING * normal[i]) * over_u + (
            sound_u * over_area
        ) * normal[i]
        slope_w = (along_w * outer_prims[1][i] + SOFTENING * normal[i]) * over_w + (
            sound_w * over_area
        ) * normal[i]
        result.append(
            0.5 * (slope_u + slope_w)
            + (difference * (slope_u - slope_w) + SOFTENING * normal[i]) * over_spread
        )
    return result


def position_bit(bit):
    return ((lax.axis_index("parts") >> bit) & 1) == 1


def pack_kernel(*refs):
    sources = refs[0:10]
    tables_hbm, damping_hbm = refs[10:12]
    (
        a_ref,
        b_ref,
        c_ref,
        d_ref,
        sends_out,
        tables_out,
        damping_out,
    ) = refs[12:19]
    held = refs[19:29]
    semaphores = refs[29]
    moves = list(zip(sources, held)) + [(tables_hbm, tables_out), (damping_hbm, damping_out)]
    copies = [
        pltpu.make_async_copy(source, target, semaphores.at[i])
        for i, (source, target) in enumerate(moves)
    ]
    for copy in copies:
        copy.start()
    for copy in copies[0:10]:
        copy.wait()
    (
        flow_ref,
        tangent_ref,
        places_ref,
        upper_ref,
        lower_ref,
        sends_ref,
        neighbour_ref,
        nodes_ref,
        flags_ref,
        far_ref,
    ) = held
    lane = lanes()
    group = lane // 32
    group16 = jnp.concatenate([group, group], axis=0)

    def faces(list_ref, row):
        index = spread(pad_lanes(list_ref[...]))
        tiled = index
        for g in range(1, 4):
            tiled = jnp.where(group == g, pltpu.roll(index, 32 * g, 1), tiled)
        chunks = []
        for first in range(0, 12, 4):
            merged = None
            for g in range(4):
                v = first + g
                if v >= 10:
                    continue
                source = flow_ref if v < 5 else tangent_ref
                block = pick(pad_lanes(source[v % 5, row : row + 16, :]), tiled)
                merged = jnp.where(group16 == g, block, 0.0 if merged is None else merged)
            chunks.append(merged)
        return jnp.concatenate(chunks, axis=0)

    up = faces(upper_ref, 48)
    down = faces(lower_ref, 0)
    sends_row = pad_lanes(sends_ref[...])
    places = pad_lanes(jnp.concatenate([places_ref[...], jnp.zeros((5, 102), F32)], axis=0))
    nodes = pick(places, spread(sends_row))
    row8 = lax.broadcasted_iota(jnp.int32, (8, 128), 0)
    nodes = jnp.where(row8 == 3, spread(sends_row.astype(F32)), nodes)
    none = jnp.zeros((8, 128), F32)
    spare = jnp.where(lane >= 64, pltpu.roll(nodes, 64, 1), down[32:40])
    down = jnp.concatenate([down[0:32], spare, down[40:48]], axis=0)

    flags = pad_lanes(flags_ref[...].astype(F32))
    first_row = lax.broadcasted_iota(jnp.int32, (64, 128), 0)
    rank = jnp.sum(
        jnp.where(lanes(64) <= first_row, jnp.broadcast_to(flags, (64, 128)), 0.0),
        axis=1,
        keepdims=True,
    )
    wanted = (lane % 16).astype(F32)
    before = jnp.sum((rank <= wanted[0:1]).astype(F32), axis=0, keepdims=True)
    weight = (before < 63.5).astype(F32)
    chosen = spread(jnp.minimum(before, 63.0).astype(jnp.int32))
    block = lane // 16

    def merged_blocks(parts):
        result = parts[0]
        for b, part in enumerate(parts[1:]):
            result = jnp.where(block == b + 1, part, result)
        return result

    neighbours = neighbour_ref[...]
    listed = [
        spread(pair(neighbours[2 * j : 2 * j + 1], neighbours[2 * j + 1 : 2 * j + 2]))
        for j in range(3)
    ]
    beside = []
    for j in range(3):
        sides = []
        for side in range(2):
            code = pick(listed[j], chosen + 64 * side)
            local = jnp.where(code < 64, code, 0) + (64 if side == 0 else 0)
            sides.append((code == 96, local))
        beside.append(sides)
    packed = []
    for v in range(5):
        value = pad_lanes(flow_ref[v])
        packed.append(
            merged_blocks([pick(value[8 * b : 8 * b + 8], chosen) for b in range(8)])
        )
    inner = [face_pairs(flow_ref, v) for v in range(5)]

    def beside_part(v, chunk, side):
        far, local = beside[chunk // 2][side]
        taken = pick(inner[v][8 * chunk : 8 * chunk + 8], local)
        return jnp.where(far, far_ref[0:1, v : v + 1], taken)

    for v in range(5):
        packed.append(merged_blocks([beside_part(v, b % 4, b // 4) for b in range(8)]))
    for first in (0, 2, 4):
        packed.append(
            merged_blocks(
                [
                    beside_part(first + b % 4 // 2, 4 + b % 2, b // 4)
                    if first + b % 4 // 2 < 5
                    else none
                    for b in range(8)
                ]
            )
        )
    node_index = pick(pair(nodes_ref[...], nodes_ref[...]), chosen)
    local_node = jnp.where(node_index < 102, node_index, 0)
    codes = jnp.where(
        row8 == 0,
        pick(listed[0], chosen).astype(F32),
        jnp.where(row8 == 1, pick(listed[0], chosen + 64).astype(F32), spread(weight)),
    )
    packed.append(
        merged_blocks(
            [pick(spread(places[i : i + 1]), local_node) for i in range(3)]
            + [node_index.astype(F32), codes]
        )
    )
    flagged = jnp.concatenate(packed, axis=0)
    sends_out[...] = sends_ref[...]
    odd = position_bit(0)
    second = position_bit(1)
    a_ref[0:48] = jnp.where(odd, down, up)
    b_ref[0:48] = jnp.where(odd, up, down)
    a_ref[48:160] = flagged
    b_ref[48:160] = flagged
    c_ref[...] = jnp.where(second, down, up)
    d_ref[...] = jnp.where(second, up, down)
    for copy in copies[10:12]:
        copy.wait()


def face_pairs(ref, v):
    value = ref[v]
    sides = []
    for s in range(2):
        first = value[48 * s : 48 * s + 16]
        second = jnp.concatenate(
            [value[16 * i + 12 * s : 16 * i + 12 * s + 4] for i in range(4)], axis=0
        )
        third = ref[pl.ds(v, 1), pl.ds(3 * s, 16, stride=4), :][0]
        sides.append(jnp.concatenate([first, second, third], axis=0))
    return pair(sides[0], sides[1])


def volume_pairs(ref, v):
    return pair(ref[v, 0:32, :], ref[v, 32:64, :])


def corner_values(index, own_rows, halo_rows):
    local = index < 102
    own_index = jnp.where(local, index, 0)
    halo_index = jnp.where(local, 0, index - 102)
    result = []
    for i in range(3):
        own = pick(spread(own_rows[i : i + 1]), own_index)
        halo = pick(spread(halo_rows[i : i + 1]), halo_index)
        result.append(jnp.where(local, own, halo))
    return result


def corner_operand(values):
    low = lanes() < 64
    blocks = [
        jnp.concatenate([jnp.where(low, v, 0.0), jnp.where(low, 0.0, v)], axis=0) for v in values
    ]
    return jnp.concatenate(blocks, axis=1)


def columns(array, rows, i):
    return array[rows, 128 * i : 128 * i + 128]


def tangents_of(spans):
    volume = [[columns(spans, slice(32 * j, 32 * j + 32), i) for i in range(3)] for j in range(3)]
    faces = [
        [columns(spans, slice(96 + 48 * w, 144 + 48 * w), i) for i in range(3)] for w in range(2)
    ]
    return volume, faces


def folded(product, v):
    block = product[:, 128 * v : 128 * v + 128]
    return block[0:64] + pltpu.roll(block[64:128], 64, 1)


def side_sign():
    return jnp.where(lanes(48) < 64, -1.0, 1.0).astype(F32)


def ready_kernel(
    flow_ref,
    tangent_ref,
    far_ref,
    places_ref,
    neighbour_ref,
    nodes_ref,
    tables_ref,
    inner_ref,
    state_ref,
    outer_ref,
    places_out,
    border_ref,
    node_index_ref,
    assemble_ref,
    corner_ref,
):
    lane = lanes()
    low = lane < 64
    neighbours = neighbour_ref[...]
    listed = [
        spread(pair(neighbours[2 * j : 2 * j + 1], neighbours[2 * j + 1 : 2 * j + 2]))
        for j in range(3)
    ]
    border_ref[...] = listed[0]
    local = []
    for j in range(3):
        index = jnp.where(listed[j] < 64, listed[j], 0)
        local.append(jnp.where(low, index + 64, index))
    far = [jnp.concatenate([m, m], axis=0) == 96 for m in listed]
    for v in range(10):
        source = flow_ref if v < 5 else tangent_ref
        inner = face_pairs(source, v % 5)
        inner_ref[v] = inner
        state_ref[v] = volume_pairs(source, v % 5)
        far_value = far_ref[0:1, v : v + 1] if v < 5 else 0.0
        for j in range(3):
            rows = slice(16 * j, 16 * j + 16)
            outer_ref[v, rows, :] = jnp.where(far[j], far_value, pick(inner[rows], local[j]))
    places_out[...] = jnp.concatenate([pad_lanes(places_ref[...]), jnp.zeros((5, 128), F32)], axis=0)
    node_index = pair(nodes_ref[...], nodes_ref[...])
    node_index_ref[...] = node_index
    assemble_ref[...] = tables_ref[0:128, 0:144]
    corner_ref[...] = tables_ref[272:472, 0:16]


class Border:
    def __init__(self, border, lower, upper):
        self.slot = jnp.clip(border - 64, 0, 31)
        halo = (border >= 64) & (border < 96)
        low = lanes() < 64
        self.below = jnp.concatenate([halo & low, halo & low], axis=0)
        self.above = jnp.concatenate([halo & ~low, halo & ~low], axis=0)
        self.lower = lower
        self.upper = upper

    def values(self, local, v):
        rows = slice(16 * (v // 4), 16 * (v // 4) + 16)
        slot = self.slot + 32 * (v % 4)
        first = jnp.where(self.below, pick(self.lower[rows], slot), local[0:16])
        first = jnp.where(self.above, pick(self.upper[rows], slot), first)
        return jnp.concatenate([first, local[16:48]], axis=0)


def geometry(volume_spans, face_spans):
    normals = [cross(volume_spans[(j + 1) % 3], volume_spans[(j + 2) % 3]) for j in range(3)]
    sign = side_sign()
    face_normal = [sign * n for n in cross(face_spans[0], face_spans[1])]
    area_square = sum(n * n for n in face_normal)
    return normals, face_normal, area_square, jnp.sqrt(area_square)


def volume_flux(state, normals):
    prims = primitives(state)
    return [along_flux(prims, normals[j]) for j in range(3)]


def assembled(assemble, fluxes, jump):
    stacked = [
        jnp.concatenate([fluxes[0][v], fluxes[1][v], fluxes[2][v], jump[v]], axis=0)
        for v in range(5)
    ]
    product = dot(assemble, jnp.concatenate(stacked, axis=1))
    return [folded(product, v) for v in range(5)]


def plane_kernel(
    inner_ref,
    state_ref,
    local_ref,
    places_ref,
    border_ref,
    node_index_ref,
    a_ref,
    b_ref,
    assemble_ref,
    corner_ref,
    residual_ref,
    change_ref,
):
    odd = position_bit(0)
    lower = jnp.where(odd, a_ref[0:48], b_ref[0:48])
    upper = jnp.where(odd, b_ref[0:48], a_ref[0:48])
    border = Border(border_ref[...], lower, upper)
    corners = corner_values(
        node_index_ref[...], places_ref[...], pltpu.roll(upper[32:40], 64, 1)
    )
    spans = dot(corner_ref[...], corner_operand([c - c[0:1] for c in corners]))
    volume_spans, face_spans = tangents_of(spans)
    normals, face_normal, area_square, area = geometry(volume_spans, face_spans)
    inner = [inner_ref[v] for v in range(10)]
    outer = [border.values(local_ref[v], v) for v in range(10)]
    jump, jump_change = jax.jvp(
        lambda u, w: jump_of(u, w, face_normal, area_square, area),
        (inner[:5], outer[:5]),
        (inner[5:], outer[5:]),
    )
    state = [state_ref[v] for v in range(10)]
    fluxes, flux_changes = jax.jvp(
        lambda u: volume_flux(u, normals), (state[:5],), (state[5:],)
    )
    residual = assembled(assemble_ref[...], fluxes, jump)
    change = assembled(assemble_ref[...], flux_changes, jump_change)
    for v in range(5):
        residual_ref[v] = residual[v][:, 0:64]
        change_ref[v] = change[v][:, 0:64]


def core_kernel(
    a_ref,
    b_ref,
    c_ref,
    d_ref,
    sent_a_ref,
    sent_b_ref,
    sends_ref,
    tables_ref,
    damping_ref,
    descent_ref,
    sums_ref,
    whole_ref,
):
    odd = position_bit(0)
    second = position_bit(1)
    lower = jnp.where(odd, a_ref[...], b_ref[...])
    upper = jnp.where(odd, b_ref[...], a_ref[...])
    lower_two = jnp.where(second, c_ref[...], d_ref[...])
    upper_two = jnp.where(second, d_ref[...], c_ref[...])
    up = jnp.where(odd, sent_b_ref[0:48], sent_a_ref[0:48])
    down = jnp.where(odd, sent_a_ref[0:48], sent_b_ref[0:48])
    flagged = sent_a_ref[48:160]
    lane = lanes()
    low = lane < 64
    seat = lane % 16
    block = (lane % 64) // 16

    def three(own, below, above):
        return jnp.where(block == 1, below, jnp.where(block == 2, above, own))

    def taken(row, index):
        rows = slice(row, row + 8)
        moved = slice(48 + row, 56 + row)
        return three(
            pick(flagged[rows], index), pick(lower[moved], index), pick(upper[moved], index)
        )

    for v in range(5):
        for r in range(8):
            whole_ref[v, 8 * r : 8 * r + 8, :] = taken(8 * v, seat + 16 * r)
    state = []
    inner = []
    for v in range(5):
        value = whole_ref[v]
        state.append(jnp.where(lanes(32) < 64, value[0:32], value[32:64]))
        sides = []
        for s in range(2):
            middle = jnp.concatenate(
                [value[16 * i + 12 * s : 16 * i + 12 * s + 4] for i in range(4)], axis=0
            )
            last = whole_ref[pl.ds(v, 1), pl.ds(3 * s, 16, stride=4), :][0]
            sides.append(jnp.concatenate([value[48 * s : 48 * s + 16], middle, last], axis=0))
        inner.append(jnp.where(lanes(48) < 64, sides[0], sides[1]))
    codes = taken(104, seat + 64)
    border = spread(jnp.where(low[0:1], codes[0:1], codes[1:2])).astype(jnp.int32)
    weight = jnp.where(block[0:1] == 3, 0.0, codes[2:3])
    slot = jnp.clip(border - 64, 0, 31)
    halo = (border >= 64) & (border < 96)
    outer = []
    for v in range(5):
        chunks = []
        for chunk in range(6):
            if chunk < 4:
                row, place = 40 + 8 * v, chunk
            else:
                row, place = 80 + 8 * (v // 2), chunk - 4 + 2 * (v % 2)
            value = taken(row, seat + 16 * place + jnp.where(low, 0, 64))
            if chunk < 2:
                rows = slice(16 * (v // 4) + 8 * chunk, 16 * (v // 4) + 8 * chunk + 8)
                at = slot + 32 * (v % 4)
                side0 = three(pick(lower[rows], at), pick(lower_two[rows], at), pick(up[rows], at))
                side1 = three(
                    pick(upper[rows], at), pick(down[rows], at), pick(upper_two[rows], at)
                )
                value = jnp.where(halo, jnp.where(low, side0, side1), value)
            chunks.append(value)
        outer.append(jnp.concatenate(chunks, axis=0))
    node_index = taken(104, seat + 48).astype(jnp.int32)
    foreign = node_index >= 102
    foreign_slot = jnp.where(foreign, node_index - 102, 0)
    corners = []
    for i in range(3):
        local = taken(104, seat + 16 * i)
        remote = three(
            pick(spread(upper[32 + i : 33 + i]), foreign_slot + 64),
            pick(spread(down[32 + i : 33 + i]), foreign_slot + 64),
            pick(spread(upper_two[32 + i : 33 + i]), foreign_slot + 64),
        )
        corners.append(jnp.where(foreign, remote, local))

    spans = dot(tables_ref[272:472, 0:16], corner_operand([c - c[0:1] for c in corners]))
    volume_spans, face_spans = tangents_of(spans)
    normals, face_normal, area_square, area = geometry(volume_spans, face_spans)
    sign = side_sign()
    jump = jump_of(inner, outer, face_normal, area_square, area)
    residual = assembled(tables_ref[0:128, 0:144], volume_flux(state, normals), jump)
    low64 = lanes(64) < 64
    seeds = []
    for v in range(5):
        seed = residual[v] * weight
        seeds.append(
            jnp.concatenate(
                [jnp.where(low64, seed, 0.0), jnp.where(low64, 0.0, pltpu.roll(seed, 64, 1))],
                axis=0,
            )
        )
    back = dot(tables_ref[128:272, 0:128], jnp.concatenate(seeds, axis=1))
    prims = primitives(state)
    normal_bar = []
    for j in range(3):
        cotangent = [columns(back, slice(32 * j, 32 * j + 32), v) for v in range(5)]
        normal_bar.append(along_flux_transposed(prims, cotangent))
    cotangent = [columns(back, slice(96, 144), v) for v in range(5)]
    inner_prims = primitives(inner)
    outer_prims = primitives(outer)
    slopes = wave_gradient(inner_prims, outer_prims, face_normal, area_square, area)
    lift = sum(c * (w - u) for c, w, u in zip(cotangent, outer, inner))
    from_outer = along_flux_transposed(outer_prims, cotangent)
    from_inner = along_flux_transposed(inner_prims, cotangent)
    face_bar = [
        (0.5 * sign) * (from_outer[i] - from_inner[i] - lift * slopes[i]) for i in range(3)
    ]
    span_bar = []
    for j in range(3):
        first = cross(volume_spans[(j + 1) % 3], normal_bar[(j + 2) % 3])
        second = cross(normal_bar[(j + 1) % 3], volume_spans[(j + 2) % 3])
        span_bar.append(added(first, second))
    face_span_bar = [cross(face_spans[1], face_bar), cross(face_bar, face_spans[0])]
    stacked_bar = jnp.concatenate(
        [
            jnp.concatenate(
                [span_bar[j][i] for j in range(3)] + [face_span_bar[w][i] for w in range(2)],
                axis=0,
            )
            for i in range(3)
        ],
        axis=1,
    )
    corner_bar = dot(tables_ref[472:488, 0:192], stacked_bar)
    smoothing = damping_ref[0:1, 1:2]
    pieces = []
    for i in range(3):
        halves = columns(corner_bar, slice(0, 16), i)
        bar = halves[0:8] + pltpu.roll(halves[8:16], 64, 1)
        bar = bar + smoothing * weight * columns(spans, slice(192, 200), i)
        pieces.append(bar)
    pieces.append(spread(weight))
    gradient = jnp.concatenate(pieces, axis=0)
    gradient = jnp.where(lanes(32) < 64, gradient, pltpu.roll(gradient, 64, 1))
    row_corner = lax.broadcasted_iota(jnp.int32, (32, 128), 0) % 8
    half = jnp.where(lanes(32) < 64, 0, 1)
    sent_here = pick(spread(pad_lanes(sends_ref[...])), foreign_slot)
    nowhere = jnp.full((8, 128), -1, jnp.int32)
    own_node = three(
        jnp.where(foreign, -1, node_index), jnp.where(foreign, sent_here, -1), nowhere
    )
    own_node = jnp.where(block == 3, -1, own_node)
    halo_node = jnp.where(block == 0, jnp.where(foreign, node_index - 102, -1), nowhere)
    upper_node = jnp.where((block == 2) & ~foreign, node_index, -1)
    square_row = lax.broadcasted_iota(jnp.int32, (128, 128), 0)
    upper_sends = jnp.where(
        lane[0:1] < 51, pltpu.roll(spread(upper[35:36]), 64, 1)[0:1], -5.0
    )
    upper_column = jnp.sum(
        jnp.where(square_row == lanes(128), jnp.broadcast_to(upper_sends, (128, 128)), 0.0),
        axis=1,
        keepdims=True,
    ).astype(jnp.int32)
    left = []
    right = []
    for p in range(4):
        left.append(jnp.where(row_corner == 2 * p + half, gradient, 0.0))

        def row_of(index):
            return jnp.where(low[0:1], index[2 * p : 2 * p + 1], index[2 * p + 1 : 2 * p + 2])

        own_hit = square_row == row_of(own_node)
        halo_hit = (square_row == row_of(halo_node)) | (upper_column == row_of(upper_node))
        right.append(
            jnp.concatenate([own_hit.astype(F32), halo_hit.astype(F32)], axis=0).astype(
                jnp.bfloat16
            )
        )
    scattered = placed(jnp.concatenate(left, axis=1), jnp.concatenate(right, axis=1))
    rows = [jnp.sum(scattered[8 * i : 8 * i + 8], axis=0, keepdims=True) for i in range(4)]
    table = jnp.concatenate(rows + [jnp.zeros((4, 256), F32)], axis=0)
    own = table[:, 0:128]
    halo_table = table[:, 128:256]
    own = -jnp.where(own[3:4] > 0.5, own, 0.0)
    halo_table = -jnp.where(halo_table[3:4] > 0.5, halo_table, 0.0)
    descent_ref[...] = own[0:3]
    moved = jnp.where(lax.broadcasted_iota(jnp.int32, (8, 128), 0) < 3, own, 0.0)
    norm = jnp.sum(moved * moved, axis=(0, 1), keepdims=True)

    steps = corner_values(node_index, own, halo_table)
    moves = dot(tables_ref[272:472, 0:16], corner_operand(steps))
    volume_moves, face_moves = tangents_of(moves)
    fluxes = []
    for j in range(3):
        a, b = (j + 1) % 3, (j + 2) % 3
        normal_move = added(
            cross(volume_moves[a], volume_spans[b]), cross(volume_spans[a], volume_moves[b])
        )
        fluxes.append(along_flux(prims, normal_move))
    face_move = [
        sign * n
        for n in added(cross(face_moves[0], face_spans[1]), cross(face_spans[0], face_moves[1]))
    ]
    inner_flux = along_flux(inner_prims, face_move)
    outer_flux = along_flux(outer_prims, face_move)
    wave_move = sum(slopes[i] * face_move[i] for i in range(3))
    jump = [
        0.5 * (outer_flux[v] - inner_flux[v] - wave_move * (outer[v] - inner[v]))
        for v in range(5)
    ]
    square = sum(change * change for change in assembled(tables_ref[0:128, 0:144], fluxes, jump))
    own_weight = jnp.where(lane[0:1] < 16, weight, 0.0)
    curvature = jnp.sum(
        jnp.sum(square, axis=0, keepdims=True) * own_weight, axis=1, keepdims=True
    )
    bend = sum(steps[i] * columns(moves, slice(192, 200), i) for i in range(3))
    bending = smoothing * jnp.sum(
        jnp.sum(bend, axis=0, keepdims=True) * own_weight, axis=1, keepdims=True
    )
    lower_sum = curvature + bending + damping_ref[0:1, 0:1] * norm
    sums = jnp.where(lane[0:1] == 0, norm, jnp.where(lane[0:1] == 1, lower_sum, 0.0))
    for i in range(sums_ref.shape[0]):
        sums_ref[i] = sums


def finish_kernel(sums_ref, descent_ref, update_ref):
    total = jnp.sum(sums_ref[...], axis=0)
    step = total[:, 0:1] / total[:, 1:2]
    update_ref[...] = step * descent_ref[:, 0:102]


def call(kernel, out_shape, arrays, cost=None, places=None, scratch=(), limit=16 << 20):
    vector = pl.BlockSpec(memory_space=pltpu.VMEM)
    return pl.pallas_call(
        kernel,
        out_shape=[
            s if isinstance(s, jax.ShapeDtypeStruct) else jax.ShapeDtypeStruct(s, F32)
            for s in out_shape
        ],
        in_specs=[pl.BlockSpec(memory_space=p) for p in places or [pltpu.VMEM] * len(arrays)],
        out_specs=[vector] * len(out_shape),
        scratch_shapes=list(scratch),
        compiler_params=pltpu.CompilerParams(vmem_limit_bytes=limit),
        cost_estimate=cost,
    )(*arrays)


def beyond(i, count):
    return (i - 1) % count if i % 2 == 0 else (i + 1) % count


def beyond_two(i, count):
    return (i - 2) % count if i // 2 % 2 == 0 else (i + 2) % count


def swapped(value, partner):
    count = lax.axis_size("parts")
    return lax.ppermute(value, "parts", [(i, partner(i)) for i in range(count)])


def stays(value):
    return pltpu.with_memory_space_constraint(value, pltpu.HBM)


def step(
    flow_state,
    state_tangent,
    far_field,
    coordinates,
    damping,
    face_neighbour,
    element_nodes,
    upper_sends,
    lower_sends,
    node_sends,
    shock_flags,
):
    count = lax.axis_size("parts")
    sends_row = node_sends.reshape(1, 51)
    flags_row = shock_flags.reshape(1, 64)
    damping_row = damping.reshape(1, 2)
    integer = jnp.int32
    tables = jnp.asarray(constant_tables())
    pack_a, pack_b, pack_c, pack_d, sends, held_tables, held_damping = call(
        pack_kernel,
        [(160, 128)] * 2
        + [(48, 128)] * 2
        + [jax.ShapeDtypeStruct((1, 51), integer), (488, 256), (1, 2)],
        tuple(
            stays(x)
            for x in (
                flow_state,
                state_tangent,
                coordinates,
                upper_sends.reshape(1, 32),
                lower_sends.reshape(1, 32),
                sends_row,
                face_neighbour,
                element_nodes,
                flags_row,
                far_field.reshape(1, 5),
                tables,
                damping_row,
            )
        ),
        places=[pltpu.HBM] * 12,
        scratch=(
            pltpu.VMEM((5, 64, 64), F32),
            pltpu.VMEM((5, 64, 64), F32),
            pltpu.VMEM((3, 102), F32),
            pltpu.VMEM((1, 32), integer),
            pltpu.VMEM((1, 32), integer),
            pltpu.VMEM((1, 51), integer),
            pltpu.VMEM((6, 64), integer),
            pltpu.VMEM((8, 64), integer),
            pltpu.VMEM((1, 64), integer),
            pltpu.VMEM((1, 5), F32),
            pltpu.SemaphoreType.DMA((12,)),
        ),
    )
    got_b = swapped(pack_b, lambda i: beyond(i, count))
    got_d = swapped(pack_d, lambda i: beyond_two(i, count))
    got_c = swapped(pack_c, lambda i: i ^ 2)
    got_a = swapped(pack_a, lambda i: i ^ 1)
    (
        inner,
        state,
        local,
        places,
        border,
        node_index,
        assemble,
        corner,
    ) = call(
        ready_kernel,
        [
            (10, 48, 128),
            (10, 32, 128),
            (10, 48, 128),
            (8, 128),
            jax.ShapeDtypeStruct((8, 128), integer),
            jax.ShapeDtypeStruct((8, 128), integer),
            (128, 144),
            (200, 16),
        ],
        (
            flow_state,
            state_tangent,
            far_field.reshape(1, 5),
            coordinates,
            face_neighbour,
            element_nodes,
            held_tables,
        ),
        pl.CostEstimate(flops=200_000_000, bytes_accessed=1_000_000, transcendentals=100_000),
    )
    group = min(16, count)
    near = [[base + g for g in range(group)] for base in range(0, count, group)]
    far = [[base + group * g for g in range(count // group)] for base in range(group)]
    descent, sums = call(
        core_kernel,
        [(3, 128), (group, 1, 128)],
        (
            got_a,
            got_b,
            got_c,
            got_d,
            pack_a,
            pack_b,
            sends,
            held_tables,
            held_damping,
        ),
        scratch=(pltpu.VMEM((5, 64, 128), F32),),
    )
    residual, change = call(
        plane_kernel,
        [(5, 64, 64)] * 2,
        (
            inner,
            state,
            local,
            places,
            border,
            node_index,
            got_a,
            got_b,
            assemble,
            corner,
        ),
        pl.CostEstimate(flops=200_000_000, bytes_accessed=1_000_000, transcendentals=100_000),
    )
    sums = lax.all_to_all(sums, "parts", 0, 0, axis_index_groups=near)
    if count > group:
        sums = jnp.broadcast_to(jnp.sum(sums, axis=0)[None], (count // group, 1, 128))
        sums = lax.all_to_all(sums, "parts", 0, 0, axis_index_groups=far)
    (update,) = call(finish_kernel, [(3, 102)], (sums, descent))
    return (residual, change, update)


def solution(mesh):
    in_specs = (
        P(None, None, "parts"),
        P(None, None, "parts"),
        P(),
        P(None, "parts"),
        P(),
        P(None, "parts"),
        P(None, "parts"),
        P("parts"),
        P("parts"),
        P("parts"),
        P("parts"),
    )
    out_specs = (P(None, None, "parts"), P(None, None, "parts"), P(None, "parts"))
    return jax.shard_map(step, mesh=mesh, in_specs=in_specs, out_specs=out_specs, check_vma=False)
```

```python
import math

import jax
import jax.numpy as jnp
import numpy as np
from jax import lax
from jax.experimental import pallas as pl
from jax.experimental.pallas import tpu as pltpu
from jax.sharding import PartitionSpec as P


GAMMA = 1.4
SOFTENING = 0.01
HIGHEST = lax.Precision.HIGHEST
HIGH = lax.Precision.HIGH
F32 = jnp.float32


def lobatto_tables():
    points = np.array([-1.0, -math.sqrt(0.2), math.sqrt(0.2), 1.0])
    weights = np.array([1.0, 5.0, 5.0, 1.0]) / 6.0
    derivative = np.zeros((4, 4))
    for a in range(4):
        for b in range(4):
            if a == b:
                derivative[a, b] = sum((1.0 / (points[a] - points[m]) for m in range(4) if m != a))
            else:
                numerator = 1.0
                denominator = 1.0
                for m in range(4):
                    if m != b:
                        denominator *= points[b] - points[m]
                        if m != a:
                            numerator *= points[a] - points[m]
                derivative[a, b] = numerator / denominator
    return (points, weights, derivative)


def shape_gradients():
    points = lobatto_tables()[0]
    gradients = np.zeros((3, 64, 8))
    for q in range(64):
        position = (q // 16, q // 4 % 4, q % 4)
        for k in range(8):
            corner_bits = (k // 4, k // 2 % 2, k % 2)
            for j in range(3):
                factor = 1.0
                for m in range(3):
                    orient = 1.0 if corner_bits[m] == 1 else -1.0
                    if m == j:
                        factor *= 0.5 * orient
                    else:
                        factor *= 0.5 * (1.0 + orient * points[position[m]])
                gradients[j, q, k] = factor
    return gradients


def edge_laplacian():
    matrix = np.zeros((8, 8))
    for k in range(8):
        matrix[k, k] = 3.0
        for b in range(3):
            matrix[k, k ^ 1 << b] = -1.0
    return matrix


def face_rows(j, s):
    rows = [q for q in range(64) if (q // 16, q // 4 % 4, q % 4)[j] == 3 * s]
    return np.array(rows)


def constant_matrices():
    _, weights, derivative = lobatto_tables()
    volume = np.einsum("a,b,c->abc", weights, weights, weights).reshape(64)
    face = np.einsum("a,b->ab", weights, weights).reshape(16)
    eye = np.eye(4)
    full = [
        np.kron(np.kron(derivative, eye), eye),
        np.kron(np.kron(eye, derivative), eye),
        np.kron(np.kron(eye, eye), derivative),
    ]
    assemble = np.zeros((128, 144))
    for half in range(2):
        rows = slice(64 * half, 64 * half + 64)
        for j in range(3):
            weighted = volume[:, None] * full[j]
            assemble[rows, 32 * j : 32 * j + 32] = weighted[:, 32 * half : 32 * half + 32]
            for point, q in enumerate(face_rows(j, half)):
                assemble[64 * half + q, 96 + 16 * j + point] = face[point]
    gradients = shape_gradients()
    corner = np.zeros((200, 16))
    for half in range(2):
        columns = slice(8 * half, 8 * half + 8)
        for j in range(3):
            corner[32 * j : 32 * j + 32, columns] = gradients[j, 32 * half : 32 * half + 32]
            for which in range(2):
                base = 96 + 48 * which + 16 * j
                corner[base : base + 16, columns] = gradients[(j + 1 + which) % 3][
                    face_rows(j, half)
                ]
    corner[192:200, 0:8] = edge_laplacian()
    return assemble.astype(np.float32), corner.astype(np.float32)


def constant_tables():
    assemble, corner = constant_matrices()
    tables = np.zeros((488, 256), np.float32)
    tables[0:128, 0:144] = assemble
    tables[128:272, 0:128] = assemble.T
    tables[272:472, 0:16] = corner
    tables[472:488, 0:192] = corner[0:192].T
    return tables


def dot(a, b, precision=HIGHEST):
    return jnp.dot(a, b, precision=precision, preferred_element_type=F32)


def placed(a, chosen):
    rows = a.shape[0]
    parts = []
    for _ in range(3):
        part = a.astype(jnp.bfloat16)
        parts.append(part)
        a = a - part.astype(F32)
    product = lax.dot_general(
        jnp.concatenate(parts, axis=0),
        chosen,
        (((1,), (1,)), ((), ())),
        preferred_element_type=F32,
    )
    return product[0:rows] + product[rows : 2 * rows] + product[2 * rows : 3 * rows]


def lanes(rows=8):
    return lax.broadcasted_iota(jnp.int32, (rows, 128), 1)


def pair(left, right):
    return jnp.concatenate([left, right], axis=1)


def pick(table, index):
    blocks = [
        jnp.take_along_axis(table[r : r + 8], index, axis=1, mode="promise_in_bounds")
        for r in range(0, table.shape[0], 8)
    ]
    return blocks[0] if len(blocks) == 1 else jnp.concatenate(blocks, axis=0)


def spread(row, rows=8):
    return jnp.broadcast_to(row, (rows, row.shape[1]))


def pad_lanes(value, width=128):
    fill = jnp.zeros((value.shape[0], width - value.shape[1]), value.dtype)
    return jnp.concatenate([value, fill], axis=1)


def primitives(values):
    density = values[0]
    momentum = values[1:4]
    energy = values[4]
    inverse = 1.0 / density
    velocity = [m * inverse for m in momentum]
    kinetic = sum(m * v for m, v in zip(momentum, velocity))
    pressure = (GAMMA - 1.0) * (energy - 0.5 * kinetic)
    return (density, velocity, pressure, momentum, energy + pressure, inverse)


def along_flux(prims, normal):
    density, velocity, pressure, momentum, total, _ = prims
    along = sum(v * n for v, n in zip(velocity, normal))
    return (
        [density * along]
        + [m * along + pressure * n for m, n in zip(momentum, normal)]
        + [total * along]
    )


def along_flux_transposed(prims, cotangent):
    density, velocity, pressure, momentum, total, _ = prims
    scale = density * cotangent[0] + total * cotangent[4]
    for m in range(3):
        scale = scale + momentum[m] * cotangent[1 + m]
    return [velocity[i] * scale + pressure * cotangent[1 + i] for i in range(3)]


def cross(a, b):
    return [
        a[1] * b[2] - a[2] * b[1],
        a[2] * b[0] - a[0] * b[2],
        a[0] * b[1] - a[1] * b[0],
    ]


def added(a, b):
    return [x + y for x, y in zip(a, b)]


def signal_speed(prims, normal, area_square, area):
    _, velocity, pressure, _, _, inverse = prims
    along = sum(v * n for v, n in zip(velocity, normal))
    root = jnp.sqrt(along * along + SOFTENING * area_square)
    sound = jnp.sqrt(GAMMA * pressure * inverse)
    return root + sound * area, along, root, sound


def jump_of(inner, outer, normal, area_square, area):
    inner_prims = primitives(inner)
    outer_prims = primitives(outer)
    inner_speed = signal_speed(inner_prims, normal, area_square, area)[0]
    outer_speed = signal_speed(outer_prims, normal, area_square, area)[0]
    difference = inner_speed - outer_speed
    wave = 0.5 * (inner_speed + outer_speed) + 0.5 * jnp.sqrt(
        difference * difference + SOFTENING * area_square
    )
    inner_flux = along_flux(inner_prims, normal)
    outer_flux = along_flux(outer_prims, normal)
    return [
        0.5 * (outer_flux[v] - inner_flux[v]) - 0.5 * wave * (outer[v] - inner[v])
        for v in range(5)
    ]


def wave_gradient(inner_prims, outer_prims, normal, area_square, area):
    inner_speed, along_u, root_u, sound_u = signal_speed(inner_prims, normal, area_square, area)
    outer_speed, along_w, root_w, sound_w = signal_speed(outer_prims, normal, area_square, area)
    difference = inner_speed - outer_speed
    spread_root = jnp.sqrt(difference * difference + SOFTENING * area_square)
    over_u = 1.0 / root_u
    over_w = 1.0 / root_w
    over_area = 1.0 / area
    over_spread = 0.5 / spread_root
    result = []
    for i in range(3):
        slope_u = (along_u * inner_prims[1][i] + SOFTENING * normal[i]) * over_u + (
            sound_u * over_area
        ) * normal[i]
        slope_w = (along_w * outer_prims[1][i] + SOFTENING * normal[i]) * over_w + (
            sound_w * over_area
        ) * normal[i]
        result.append(
            0.5 * (slope_u + slope_w)
            + (difference * (slope_u - slope_w) + SOFTENING * normal[i]) * over_spread
        )
    return result


def position_bit(bit):
    return ((lax.axis_index("parts") >> bit) & 1) == 1


def pack_kernel(*refs):
    sources = refs[0:10]
    tables_hbm, damping_hbm = refs[10:12]
    (
        a_ref,
        b_ref,
        c_ref,
        d_ref,
        sends_out,
        tables_out,
        damping_out,
    ) = refs[12:19]
    held = refs[19:29]
    semaphores = refs[29]
    moves = list(zip(sources, held)) + [(tables_hbm, tables_out), (damping_hbm, damping_out)]
    copies = [
        pltpu.make_async_copy(source, target, semaphores.at[i])
        for i, (source, target) in enumerate(moves)
    ]
    for copy in copies:
        copy.start()
    for copy in copies[0:10]:
        copy.wait()
    (
        flow_ref,
        tangent_ref,
        places_ref,
        upper_ref,
        lower_ref,
        sends_ref,
        neighbour_ref,
        nodes_ref,
        flags_ref,
        far_ref,
    ) = held
    lane = lanes()
    group = lane // 32
    group16 = jnp.concatenate([group, group], axis=0)

    def faces(list_ref, row):
        index = spread(pad_lanes(list_ref[...]))
        tiled = index
        for g in range(1, 4):
            tiled = jnp.where(group == g, pltpu.roll(index, 32 * g, 1), tiled)
        chunks = []
        for first in range(0, 12, 4):
            merged = None
            for g in range(4):
                v = first + g
                if v >= 10:
                    continue
                source = flow_ref if v < 5 else tangent_ref
                block = pick(pad_lanes(source[v % 5, row : row + 16, :]), tiled)
                merged = jnp.where(group16 == g, block, 0.0 if merged is None else merged)
            chunks.append(merged)
        return jnp.concatenate(chunks, axis=0)

    up = faces(upper_ref, 48)
    down = faces(lower_ref, 0)
    sends_row = pad_lanes(sends_ref[...])
    places = pad_lanes(jnp.concatenate([places_ref[...], jnp.zeros((5, 102), F32)], axis=0))
    nodes = pick(places, spread(sends_row))
    row8 = lax.broadcasted_iota(jnp.int32, (8, 128), 0)
    nodes = jnp.where(row8 == 3, spread(sends_row.astype(F32)), nodes)
    none = jnp.zeros((8, 128), F32)
    spare = jnp.where(lane >= 64, pltpu.roll(nodes, 64, 1), down[32:40])
    down = jnp.concatenate([down[0:32], spare, down[40:48]], axis=0)

    flags = pad_lanes(flags_ref[...].astype(F32))
    first_row = lax.broadcasted_iota(jnp.int32, (64, 128), 0)
    rank = jnp.sum(
        jnp.where(lanes(64) <= first_row, jnp.broadcast_to(flags, (64, 128)), 0.0),
        axis=1,
        keepdims=True,
    )
    wanted = (lane % 16).astype(F32)
    before = jnp.sum((rank <= wanted[0:1]).astype(F32), axis=0, keepdims=True)
    weight = (before < 63.5).astype(F32)
    chosen = spread(jnp.minimum(before, 63.0).astype(jnp.int32))
    block = lane // 16

    def merged_blocks(parts):
        result = parts[0]
        for b, part in enumerate(parts[1:]):
            result = jnp.where(block == b + 1, part, result)
        return result

    neighbours = neighbour_ref[...]
    listed = [
        spread(pair(neighbours[2 * j : 2 * j + 1], neighbours[2 * j + 1 : 2 * j + 2]))
        for j in range(3)
    ]
    beside = []
    for j in range(3):
        sides = []
        for side in range(2):
            code = pick(listed[j], chosen + 64 * side)
            local = jnp.where(code < 64, code, 0) + (64 if side == 0 else 0)
            sides.append((code == 96, local))
        beside.append(sides)
    packed = []
    for v in range(5):
        value = pad_lanes(flow_ref[v])
        packed.append(
            merged_blocks([pick(value[8 * b : 8 * b + 8], chosen) for b in range(8)])
        )
    inner = [face_pairs(flow_ref, v) for v in range(5)]

    def beside_part(v, chunk, side):
        far, local = beside[chunk // 2][side]
        taken = pick(inner[v][8 * chunk : 8 * chunk + 8], local)
        return jnp.where(far, far_ref[0:1, v : v + 1], taken)

    for v in range(5):
        packed.append(merged_blocks([beside_part(v, b % 4, b // 4) for b in range(8)]))
    for first in (0, 2, 4):
        packed.append(
            merged_blocks(
                [
                    beside_part(first + b % 4 // 2, 4 + b % 2, b // 4)
                    if first + b % 4 // 2 < 5
                    else none
                    for b in range(8)
                ]
            )
        )
    node_index = pick(pair(nodes_ref[...], nodes_ref[...]), chosen)
    local_node = jnp.where(node_index < 102, node_index, 0)
    codes = jnp.where(
        row8 == 0,
        pick(listed[0], chosen).astype(F32),
        jnp.where(row8 == 1, pick(listed[0], chosen + 64).astype(F32), spread(weight)),
    )
    packed.append(
        merged_blocks(
            [pick(spread(places[i : i + 1]), local_node) for i in range(3)]
            + [node_index.astype(F32), codes]
        )
    )
    flagged = jnp.concatenate(packed, axis=0)
    sends_out[...] = sends_ref[...]
    odd = position_bit(0)
    second = position_bit(1)
    a_ref[0:48] = jnp.where(odd, down, up)
    b_ref[0:48] = jnp.where(odd, up, down)
    a_ref[48:160] = flagged
    b_ref[48:160] = flagged
    c_ref[...] = jnp.where(second, down, up)
    d_ref[...] = jnp.where(second, up, down)
    for copy in copies[10:12]:
        copy.wait()


def face_pairs(ref, v):
    value = ref[v]
    sides = []
    for s in range(2):
        first = value[48 * s : 48 * s + 16]
        second = jnp.concatenate(
            [value[16 * i + 12 * s : 16 * i + 12 * s + 4] for i in range(4)], axis=0
        )
        third = ref[pl.ds(v, 1), pl.ds(3 * s, 16, stride=4), :][0]
        sides.append(jnp.concatenate([first, second, third], axis=0))
    return pair(sides[0], sides[1])


def volume_pairs(ref, v):
    return pair(ref[v, 0:32, :], ref[v, 32:64, :])


def corner_values(index, own_rows, halo_rows):
    local = index < 102
    own_index = jnp.where(local, index, 0)
    halo_index = jnp.where(local, 0, index - 102)
    result = []
    for i in range(3):
        own = pick(spread(own_rows[i : i + 1]), own_index)
        halo = pick(spread(halo_rows[i : i + 1]), halo_index)
        result.append(jnp.where(local, own, halo))
    return result


def corner_operand(values):
    low = lanes() < 64
    blocks = [
        jnp.concatenate([jnp.where(low, v, 0.0), jnp.where(low, 0.0, v)], axis=0) for v in values
    ]
    return jnp.concatenate(blocks, axis=1)


def columns(array, rows, i):
    return array[rows, 128 * i : 128 * i + 128]


def tangents_of(spans):
    volume = [[columns(spans, slice(32 * j, 32 * j + 32), i) for i in range(3)] for j in range(3)]
    faces = [
        [columns(spans, slice(96 + 48 * w, 144 + 48 * w), i) for i in range(3)] for w in range(2)
    ]
    return volume, faces


def folded(product, v):
    block = product[:, 128 * v : 128 * v + 128]
    return block[0:64] + pltpu.roll(block[64:128], 64, 1)


def side_sign():
    return jnp.where(lanes(48) < 64, -1.0, 1.0).astype(F32)


def ready_kernel(
    flow_ref,
    tangent_ref,
    far_ref,
    places_ref,
    neighbour_ref,
    nodes_ref,
    tables_ref,
    inner_ref,
    state_ref,
    outer_ref,
    places_out,
    border_ref,
    node_index_ref,
    assemble_ref,
    corner_ref,
):
    lane = lanes()
    low = lane < 64
    neighbours = neighbour_ref[...]
    listed = [
        spread(pair(neighbours[2 * j : 2 * j + 1], neighbours[2 * j + 1 : 2 * j + 2]))
        for j in range(3)
    ]
    border_ref[...] = listed[0]
    local = []
    for j in range(3):
        index = jnp.where(listed[j] < 64, listed[j], 0)
        local.append(jnp.where(low, index + 64, index))
    far = [jnp.concatenate([m, m], axis=0) == 96 for m in listed]
    for v in range(10):
        source = flow_ref if v < 5 else tangent_ref
        inner = face_pairs(source, v % 5)
        inner_ref[v] = inner
        state_ref[v] = volume_pairs(source, v % 5)
        far_value = far_ref[0:1, v : v + 1] if v < 5 else 0.0
        for j in range(3):
            rows = slice(16 * j, 16 * j + 16)
            outer_ref[v, rows, :] = jnp.where(far[j], far_value, pick(inner[rows], local[j]))
    places_out[...] = jnp.concatenate([pad_lanes(places_ref[...]), jnp.zeros((5, 128), F32)], axis=0)
    node_index = pair(nodes_ref[...], nodes_ref[...])
    node_index_ref[...] = node_index
    assemble_ref[...] = tables_ref[0:128, 0:144]
    corner_ref[...] = tables_ref[272:472, 0:16]


class Border:
    def __init__(self, border, lower, upper):
        self.slot = jnp.clip(border - 64, 0, 31)
        halo = (border >= 64) & (border < 96)
        low = lanes() < 64
        self.below = jnp.concatenate([halo & low, halo & low], axis=0)
        self.above = jnp.concatenate([halo & ~low, halo & ~low], axis=0)
        self.lower = lower
        self.upper = upper

    def values(self, local, v):
        rows = slice(16 * (v // 4), 16 * (v // 4) + 16)
        slot = self.slot + 32 * (v % 4)
        first = jnp.where(self.below, pick(self.lower[rows], slot), local[0:16])
        first = jnp.where(self.above, pick(self.upper[rows], slot), first)
        return jnp.concatenate([first, local[16:48]], axis=0)


def geometry(volume_spans, face_spans):
    normals = [cross(volume_spans[(j + 1) % 3], volume_spans[(j + 2) % 3]) for j in range(3)]
    sign = side_sign()
    face_normal = [sign * n for n in cross(face_spans[0], face_spans[1])]
    area_square = sum(n * n for n in face_normal)
    return normals, face_normal, area_square, jnp.sqrt(area_square)


def volume_flux(state, normals):
    prims = primitives(state)
    return [along_flux(prims, normals[j]) for j in range(3)]


def assembled(assemble, fluxes, jump, precision=HIGHEST):
    stacked = [
        jnp.concatenate([fluxes[0][v], fluxes[1][v], fluxes[2][v], jump[v]], axis=0)
        for v in range(5)
    ]
    product = dot(assemble, jnp.concatenate(stacked, axis=1), precision)
    return [folded(product, v) for v in range(5)]


def plane_kernel(
    inner_ref,
    state_ref,
    local_ref,
    places_ref,
    border_ref,
    node_index_ref,
    a_ref,
    b_ref,
    assemble_ref,
    corner_ref,
    residual_ref,
    change_ref,
):
    odd = position_bit(0)
    lower = jnp.where(odd, a_ref[0:48], b_ref[0:48])
    upper = jnp.where(odd, b_ref[0:48], a_ref[0:48])
    border = Border(border_ref[...], lower, upper)
    corners = corner_values(
        node_index_ref[...], places_ref[...], pltpu.roll(upper[32:40], 64, 1)
    )
    spans = dot(corner_ref[...], corner_operand([c - c[0:1] for c in corners]))
    volume_spans, face_spans = tangents_of(spans)
    normals, face_normal, area_square, area = geometry(volume_spans, face_spans)
    inner = [inner_ref[v] for v in range(10)]
    outer = [border.values(local_ref[v], v) for v in range(10)]
    jump, jump_change = jax.jvp(
        lambda u, w: jump_of(u, w, face_normal, area_square, area),
        (inner[:5], outer[:5]),
        (inner[5:], outer[5:]),
    )
    state = [state_ref[v] for v in range(10)]
    fluxes, flux_changes = jax.jvp(
        lambda u: volume_flux(u, normals), (state[:5],), (state[5:],)
    )
    residual = assembled(assemble_ref[...], fluxes, jump)
    change = assembled(assemble_ref[...], flux_changes, jump_change)
    for v in range(5):
        residual_ref[v] = residual[v][:, 0:64]
        change_ref[v] = change[v][:, 0:64]


def core_kernel(
    a_ref,
    b_ref,
    c_ref,
    d_ref,
    sent_a_ref,
    sent_b_ref,
    sends_ref,
    tables_ref,
    damping_ref,
    descent_ref,
    sums_ref,
    whole_ref,
):
    odd = position_bit(0)
    second = position_bit(1)
    lower = jnp.where(odd, a_ref[...], b_ref[...])
    upper = jnp.where(odd, b_ref[...], a_ref[...])
    lower_two = jnp.where(second, c_ref[...], d_ref[...])
    upper_two = jnp.where(second, d_ref[...], c_ref[...])
    up = jnp.where(odd, sent_b_ref[0:48], sent_a_ref[0:48])
    down = jnp.where(odd, sent_a_ref[0:48], sent_b_ref[0:48])
    flagged = sent_a_ref[48:160]
    lane = lanes()
    low = lane < 64
    seat = lane % 16
    block = (lane % 64) // 16

    def three(own, below, above):
        return jnp.where(block == 1, below, jnp.where(block == 2, above, own))

    def taken(row, index):
        rows = slice(row, row + 8)
        moved = slice(48 + row, 56 + row)
        return three(
            pick(flagged[rows], index), pick(lower[moved], index), pick(upper[moved], index)
        )

    for v in range(5):
        for r in range(8):
            whole_ref[v, 8 * r : 8 * r + 8, :] = taken(8 * v, seat + 16 * r)
    state = []
    inner = []
    for v in range(5):
        value = whole_ref[v]
        state.append(jnp.where(lanes(32) < 64, value[0:32], value[32:64]))
        sides = []
        for s in range(2):
            middle = jnp.concatenate(
                [value[16 * i + 12 * s : 16 * i + 12 * s + 4] for i in range(4)], axis=0
            )
            last = whole_ref[pl.ds(v, 1), pl.ds(3 * s, 16, stride=4), :][0]
            sides.append(jnp.concatenate([value[48 * s : 48 * s + 16], middle, last], axis=0))
        inner.append(jnp.where(lanes(48) < 64, sides[0], sides[1]))
    codes = taken(104, seat + 64)
    border = spread(jnp.where(low[0:1], codes[0:1], codes[1:2])).astype(jnp.int32)
    weight = jnp.where(block[0:1] == 3, 0.0, codes[2:3])
    slot = jnp.clip(border - 64, 0, 31)
    halo = (border >= 64) & (border < 96)
    outer = []
    for v in range(5):
        chunks = []
        for chunk in range(6):
            if chunk < 4:
                row, place = 40 + 8 * v, chunk
            else:
                row, place = 80 + 8 * (v // 2), chunk - 4 + 2 * (v % 2)
            value = taken(row, seat + 16 * place + jnp.where(low, 0, 64))
            if chunk < 2:
                rows = slice(16 * (v // 4) + 8 * chunk, 16 * (v // 4) + 8 * chunk + 8)
                at = slot + 32 * (v % 4)
                side0 = three(pick(lower[rows], at), pick(lower_two[rows], at), pick(up[rows], at))
                side1 = three(
                    pick(upper[rows], at), pick(down[rows], at), pick(upper_two[rows], at)
                )
                value = jnp.where(halo, jnp.where(low, side0, side1), value)
            chunks.append(value)
        outer.append(jnp.concatenate(chunks, axis=0))
    node_index = taken(104, seat + 48).astype(jnp.int32)
    foreign = node_index >= 102
    foreign_slot = jnp.where(foreign, node_index - 102, 0)
    corners = []
    for i in range(3):
        local = taken(104, seat + 16 * i)
        remote = three(
            pick(spread(upper[32 + i : 33 + i]), foreign_slot + 64),
            pick(spread(down[32 + i : 33 + i]), foreign_slot + 64),
            pick(spread(upper_two[32 + i : 33 + i]), foreign_slot + 64),
        )
        corners.append(jnp.where(foreign, remote, local))

    spans = dot(tables_ref[272:472, 0:16], corner_operand([c - c[0:1] for c in corners]))
    volume_spans, face_spans = tangents_of(spans)
    normals, face_normal, area_square, area = geometry(volume_spans, face_spans)
    sign = side_sign()
    jump = jump_of(inner, outer, face_normal, area_square, area)
    residual = assembled(tables_ref[0:128, 0:144], volume_flux(state, normals), jump)
    low64 = lanes(64) < 64
    seeds = []
    for v in range(5):
        seed = residual[v] * weight
        seeds.append(
            jnp.concatenate(
                [jnp.where(low64, seed, 0.0), jnp.where(low64, 0.0, pltpu.roll(seed, 64, 1))],
                axis=0,
            )
        )
    back = dot(tables_ref[128:272, 0:128], jnp.concatenate(seeds, axis=1), HIGH)
    prims = primitives(state)
    normal_bar = []
    for j in range(3):
        cotangent = [columns(back, slice(32 * j, 32 * j + 32), v) for v in range(5)]
        normal_bar.append(along_flux_transposed(prims, cotangent))
    cotangent = [columns(back, slice(96, 144), v) for v in range(5)]
    inner_prims = primitives(inner)
    outer_prims = primitives(outer)
    slopes = wave_gradient(inner_prims, outer_prims, face_normal, area_square, area)
    lift = sum(c * (w - u) for c, w, u in zip(cotangent, outer, inner))
    from_outer = along_flux_transposed(outer_prims, cotangent)
    from_inner = along_flux_transposed(inner_prims, cotangent)
    face_bar = [
        (0.5 * sign) * (from_outer[i] - from_inner[i] - lift * slopes[i]) for i in range(3)
    ]
    span_bar = []
    for j in range(3):
        first = cross(volume_spans[(j + 1) % 3], normal_bar[(j + 2) % 3])
        second = cross(normal_bar[(j + 1) % 3], volume_spans[(j + 2) % 3])
        span_bar.append(added(first, second))
    face_span_bar = [cross(face_spans[1], face_bar), cross(face_bar, face_spans[0])]
    stacked_bar = jnp.concatenate(
        [
            jnp.concatenate(
                [span_bar[j][i] for j in range(3)] + [face_span_bar[w][i] for w in range(2)],
                axis=0,
            )
            for i in range(3)
        ],
        axis=1,
    )
    corner_bar = dot(tables_ref[472:488, 0:192], stacked_bar, HIGH)
    smoothing = damping_ref[0:1, 1:2]
    pieces = []
    for i in range(3):
        halves = columns(corner_bar, slice(0, 16), i)
        bar = halves[0:8] + pltpu.roll(halves[8:16], 64, 1)
        bar = bar + smoothing * weight * columns(spans, slice(192, 200), i)
        pieces.append(bar)
    pieces.append(spread(weight))
    gradient = jnp.concatenate(pieces, axis=0)
    gradient = jnp.where(lanes(32) < 64, gradient, pltpu.roll(gradient, 64, 1))
    row_corner = lax.broadcasted_iota(jnp.int32, (32, 128), 0) % 8
    half = jnp.where(lanes(32) < 64, 0, 1)
    sent_here = pick(spread(pad_lanes(sends_ref[...])), foreign_slot)
    nowhere = jnp.full((8, 128), -1, jnp.int32)
    own_node = three(
        jnp.where(foreign, -1, node_index), jnp.where(foreign, sent_here, -1), nowhere
    )
    own_node = jnp.where(block == 3, -1, own_node)
    halo_node = jnp.where(block == 0, jnp.where(foreign, node_index - 102, -1), nowhere)
    upper_node = jnp.where((block == 2) & ~foreign, node_index, -1)
    square_row = lax.broadcasted_iota(jnp.int32, (128, 128), 0)
    upper_sends = jnp.where(
        lane[0:1] < 51, pltpu.roll(spread(upper[35:36]), 64, 1)[0:1], -5.0
    )
    upper_column = jnp.sum(
        jnp.where(square_row == lanes(128), jnp.broadcast_to(upper_sends, (128, 128)), 0.0),
        axis=1,
        keepdims=True,
    ).astype(jnp.int32)
    left = []
    right = []
    for p in range(4):
        left.append(jnp.where(row_corner == 2 * p + half, gradient, 0.0))

        def row_of(index):
            return jnp.where(low[0:1], index[2 * p : 2 * p + 1], index[2 * p + 1 : 2 * p + 2])

        own_hit = square_row == row_of(own_node)
        halo_hit = (square_row == row_of(halo_node)) | (upper_column == row_of(upper_node))
        right.append(
            jnp.concatenate([own_hit.astype(F32), halo_hit.astype(F32)], axis=0).astype(
                jnp.bfloat16
            )
        )
    scattered = placed(jnp.concatenate(left, axis=1), jnp.concatenate(right, axis=1))
    rows = [jnp.sum(scattered[8 * i : 8 * i + 8], axis=0, keepdims=True) for i in range(4)]
    table = jnp.concatenate(rows + [jnp.zeros((4, 256), F32)], axis=0)
    own = table[:, 0:128]
    halo_table = table[:, 128:256]
    own = -jnp.where(own[3:4] > 0.5, own, 0.0)
    halo_table = -jnp.where(halo_table[3:4] > 0.5, halo_table, 0.0)
    descent_ref[...] = own[0:3]
    moved = jnp.where(lax.broadcasted_iota(jnp.int32, (8, 128), 0) < 3, own, 0.0)
    norm = jnp.sum(moved * moved, axis=(0, 1), keepdims=True)

    steps = corner_values(node_index, own, halo_table)
    moves = dot(tables_ref[272:472, 0:16], corner_operand(steps), HIGH)
    volume_moves, face_moves = tangents_of(moves)
    fluxes = []
    for j in range(3):
        a, b = (j + 1) % 3, (j + 2) % 3
        normal_move = added(
            cross(volume_moves[a], volume_spans[b]), cross(volume_spans[a], volume_moves[b])
        )
        fluxes.append(along_flux(prims, normal_move))
    face_move = [
        sign * n
        for n in added(cross(face_moves[0], face_spans[1]), cross(face_spans[0], face_moves[1]))
    ]
    inner_flux = along_flux(inner_prims, face_move)
    outer_flux = along_flux(outer_prims, face_move)
    wave_move = sum(slopes[i] * face_move[i] for i in range(3))
    jump = [
        0.5 * (outer_flux[v] - inner_flux[v] - wave_move * (outer[v] - inner[v]))
        for v in range(5)
    ]
    square = sum(change * change for change in assembled(tables_ref[0:128, 0:144], fluxes, jump, HIGH))
    own_weight = jnp.where(lane[0:1] < 16, weight, 0.0)
    curvature = jnp.sum(
        jnp.sum(square, axis=0, keepdims=True) * own_weight, axis=1, keepdims=True
    )
    bend = sum(steps[i] * columns(moves, slice(192, 200), i) for i in range(3))
    bending = smoothing * jnp.sum(
        jnp.sum(bend, axis=0, keepdims=True) * own_weight, axis=1, keepdims=True
    )
    lower_sum = curvature + bending + damping_ref[0:1, 0:1] * norm
    sums = jnp.where(lane[0:1] == 0, norm, jnp.where(lane[0:1] == 1, lower_sum, 0.0))
    for i in range(sums_ref.shape[0]):
        sums_ref[i] = sums


def finish_kernel(sums_ref, descent_ref, update_ref):
    total = jnp.sum(sums_ref[...], axis=0)
    step = total[:, 0:1] / total[:, 1:2]
    update_ref[...] = step * descent_ref[:, 0:102]


def call(kernel, out_shape, arrays, cost=None, places=None, scratch=(), limit=16 << 20):
    vector = pl.BlockSpec(memory_space=pltpu.VMEM)
    return pl.pallas_call(
        kernel,
        out_shape=[
            s if isinstance(s, jax.ShapeDtypeStruct) else jax.ShapeDtypeStruct(s, F32)
            for s in out_shape
        ],
        in_specs=[pl.BlockSpec(memory_space=p) for p in places or [pltpu.VMEM] * len(arrays)],
        out_specs=[vector] * len(out_shape),
        scratch_shapes=list(scratch),
        compiler_params=pltpu.CompilerParams(vmem_limit_bytes=limit),
        cost_estimate=cost,
    )(*arrays)


def beyond(i, count):
    return (i - 1) % count if i % 2 == 0 else (i + 1) % count


def beyond_two(i, count):
    return (i - 2) % count if i // 2 % 2 == 0 else (i + 2) % count


def swapped(value, partner):
    count = lax.axis_size("parts")
    return lax.ppermute(value, "parts", [(i, partner(i)) for i in range(count)])


def stays(value):
    return pltpu.with_memory_space_constraint(value, pltpu.HBM)


def step(
    flow_state,
    state_tangent,
    far_field,
    coordinates,
    damping,
    face_neighbour,
    element_nodes,
    upper_sends,
    lower_sends,
    node_sends,
    shock_flags,
):
    count = lax.axis_size("parts")
    sends_row = node_sends.reshape(1, 51)
    flags_row = shock_flags.reshape(1, 64)
    damping_row = damping.reshape(1, 2)
    integer = jnp.int32
    tables = jnp.asarray(constant_tables())
    pack_a, pack_b, pack_c, pack_d, sends, held_tables, held_damping = call(
        pack_kernel,
        [(160, 128)] * 2
        + [(48, 128)] * 2
        + [jax.ShapeDtypeStruct((1, 51), integer), (488, 256), (1, 2)],
        tuple(
            stays(x)
            for x in (
                flow_state,
                state_tangent,
                coordinates,
                upper_sends.reshape(1, 32),
                lower_sends.reshape(1, 32),
                sends_row,
                face_neighbour,
                element_nodes,
                flags_row,
                far_field.reshape(1, 5),
                tables,
                damping_row,
            )
        ),
        places=[pltpu.HBM] * 12,
        scratch=(
            pltpu.VMEM((5, 64, 64), F32),
            pltpu.VMEM((5, 64, 64), F32),
            pltpu.VMEM((3, 102), F32),
            pltpu.VMEM((1, 32), integer),
            pltpu.VMEM((1, 32), integer),
            pltpu.VMEM((1, 51), integer),
            pltpu.VMEM((6, 64), integer),
            pltpu.VMEM((8, 64), integer),
            pltpu.VMEM((1, 64), integer),
            pltpu.VMEM((1, 5), F32),
            pltpu.SemaphoreType.DMA((12,)),
        ),
    )
    got_b = swapped(pack_b, lambda i: beyond(i, count))
    got_d = swapped(pack_d, lambda i: beyond_two(i, count))
    got_c = swapped(pack_c, lambda i: i ^ 2)
    got_a = swapped(pack_a, lambda i: i ^ 1)
    (
        inner,
        state,
        local,
        places,
        border,
        node_index,
        assemble,
        corner,
    ) = call(
        ready_kernel,
        [
            (10, 48, 128),
            (10, 32, 128),
            (10, 48, 128),
            (8, 128),
            jax.ShapeDtypeStruct((8, 128), integer),
            jax.ShapeDtypeStruct((8, 128), integer),
            (128, 144),
            (200, 16),
        ],
        (
            flow_state,
            state_tangent,
            far_field.reshape(1, 5),
            coordinates,
            face_neighbour,
            element_nodes,
            held_tables,
        ),
        pl.CostEstimate(flops=200_000_000, bytes_accessed=1_000_000, transcendentals=100_000),
    )
    group = min(16, count)
    near = [[base + g for g in range(group)] for base in range(0, count, group)]
    far = [[base + group * g for g in range(count // group)] for base in range(group)]
    descent, sums = call(
        core_kernel,
        [(3, 128), (group, 1, 128)],
        (
            got_a,
            got_b,
            got_c,
            got_d,
            pack_a,
            pack_b,
            sends,
            held_tables,
            held_damping,
        ),
        scratch=(pltpu.VMEM((5, 64, 128), F32),),
    )
    residual, change = call(
        plane_kernel,
        [(5, 64, 64)] * 2,
        (
            inner,
            state,
            local,
            places,
            border,
            node_index,
            got_a,
            got_b,
            assemble,
            corner,
        ),
        pl.CostEstimate(flops=200_000_000, bytes_accessed=1_000_000, transcendentals=100_000),
    )
    sums = lax.all_to_all(sums, "parts", 0, 0, axis_index_groups=near)
    if count > group:
        sums = jnp.broadcast_to(jnp.sum(sums, axis=0)[None], (count // group, 1, 128))
        sums = lax.all_to_all(sums, "parts", 0, 0, axis_index_groups=far)
    (update,) = call(finish_kernel, [(3, 102)], (sums, descent))
    return (residual, change, update)


def solution(mesh):
    in_specs = (
        P(None, None, "parts"),
        P(None, None, "parts"),
        P(),
        P(None, "parts"),
        P(),
        P(None, "parts"),
        P(None, "parts"),
        P("parts"),
        P("parts"),
        P("parts"),
        P("parts"),
    )
    out_specs = (P(None, None, "parts"), P(None, None, "parts"), P(None, "parts"))
    return jax.shard_map(step, mesh=mesh, in_specs=in_specs, out_specs=out_specs, check_vma=False)
```
